512 devices in a mesh: blk: 16 (over z), pen: 32 (over x, y, core).
Axes of the slice: x: 4, y: 4, z: 16, core: 2. Of those that a mesh axis runs over, the one named last changes fastest.
Arguments:
- state: bfloat16 [16, 2, 32, 512, 512], P('blk', None, None, 'pen'), may hold values from -6 to 6
- inverse_x: bfloat16 [16, 2, 512, 512], P('blk')
- inverse_y: bfloat16 [16, 2, 512, 512], P('blk')
- rates: float32 [16, 3], P('blk'), may hold values from 0.05 to 0.4
- partner: int32 [16, 2], P('blk'), may hold values from 0 to 15
- face_side: int32 [16, 2], P('blk'), may hold values from 0 to 1
- orient: int32 [16, 2], P('blk'), may hold values from 0 to 1
- offset: int32 [16, 2], P('blk'), may hold values from 0 to 31
Outputs:
- relaxed: bfloat16 [16, 2, 32, 512, 512], P('blk', None, None, 'pen')
The draws below stay inside these ranges and needn't reach their ends.
All inputs are finite; a program needn't handle non-finite values.
Results may differ from the reference program's by a relative error of at most 0.0058.
Values may be sent and summed in bfloat16 or wider, within the bound.
No kernel may reach another device: no remote copies, remote signals or barrier semaphores. Data moves between devices by JAX's collectives and lax.ppermute only.
A program may use at most 64 MiB of HBM per device.

```python
import math
import jax
import jax.numpy as jnp
from jax import lax

GX = 512
GY = 512
GZ = 32
STEPS = 2
NB = 16
ROWS = 16
N_PEN = 32


def draw_inverse_x(key, part):
    k_diag, k_off = jax.random.split(jax.random.fold_in(key, 11))
    diagonal = jax.random.uniform(k_diag, (NB, 2, GX), jnp.float32, 0.6, 1.2)
    spread_off = jax.random.normal(k_off, (NB, 2, GX, GX), jnp.float32) * (0.5 / math.sqrt(GX))
    identity = jnp.eye(GX, dtype=jnp.float32)
    return (spread_off * (1.0 - identity) + diagonal[..., None] * identity).astype(jnp.bfloat16)


def draw_inverse_y(key, part):
    k_diag, k_off = jax.random.split(jax.random.fold_in(key, 23))
    diagonal = jax.random.uniform(k_diag, (NB, 2, GY), jnp.float32, 0.6, 1.2)
    spread_off = jax.random.normal(k_off, (NB, 2, GY, GY), jnp.float32) * (0.5 / math.sqrt(GY))
    identity = jnp.eye(GY, dtype=jnp.float32)
    return (spread_off * (1.0 - identity) + diagonal[..., None] * identity).astype(jnp.bfloat16)


def plant(array, stream_key, least, largest):
    place = [jax.random.randint(jax.random.fold_in(stream_key, axis), (), 0, length) for axis, length in enumerate(array.shape)]
    longest = array.shape.index(max(array.shape))
    neighbour = place[:longest] + [(place[longest] + 1) % array.shape[longest]] + place[longest + 1:]
    return array.at[tuple(place)].set(least).at[tuple(neighbour)].set(largest)


def block_scale(rng, dims, cuts, least, high):
    def one(axis_at, shards_of):
        heights = jax.random.uniform(jax.random.fold_in(jax.random.fold_in(rng, 6), axis_at), (shards_of,), jnp.float32, least / len(cuts), high / len(cuts))
        return jnp.repeat(jnp.exp(heights), dims[axis_at] // shards_of).reshape((-1,) + (1,) * (len(dims) - axis_at - 1))

    factor_of = one(*cuts[0])
    for cut in cuts[1:]:
        factor_of = factor_of * one(*cut)
    return factor_of


def noise(key, dims, spread, limit, shards=(), held_as=jnp.bfloat16):
    array = jax.random.normal(key, dims, jnp.float32) * spread
    if len(shards) > 0:
        array = block_scale(key, dims, shards, -0.22, 0.18) * array
    return jnp.clip(array, min=-limit, max=limit).astype(held_as)


def setup_inputs(seed: int = 0) -> dict:
    splits = jax.random.split(jax.random.key(seed), 9)
    return {
        "state": noise(splits[0], (NB, 2, GZ, GY, GX), 1.0, 6.0, ((0, 16), (3, 32))),
        "inverse_x": draw_inverse_x(jax.random.fold_in(splits[8], 71), 0),
        "inverse_y": draw_inverse_y(jax.random.fold_in(splits[8], 71), 0),
        "rates": jnp.clip(jnp.exp(math.log(0.4) - 2.0794415 * jax.random.uniform(splits[3], (NB, 3), jnp.float32) ** block_scale(splits[3], (NB, 3), ((0, 16),), -0.2, 0.2)), 0.05, 0.4),
        "partner": plant(jax.random.randint(splits[4], (NB, 2), 0, NB), jax.random.fold_in(splits[4], 1), 0, NB - 1).astype(jnp.int32),
        "face_side": plant(jax.random.randint(splits[5], (NB, 2), 0, 2), jax.random.fold_in(splits[5], 1), 0, 1).astype(jnp.int32),
        "orient": plant(jax.random.randint(splits[6], (NB, 2), 0, 2), jax.random.fold_in(splits[6], 1), 0, 1).astype(jnp.int32),
        "offset": plant(jax.random.randint(splits[7], (NB, 2), 0, N_PEN), jax.random.fold_in(splits[7], 1), 0, N_PEN - 1).astype(jnp.int32),
    }


def reference(state, inverse_x, inverse_y, rates, partner, face_side, orient, offset):
    rows_y = jnp.arange(GY, dtype=jnp.int32)
    magnet = state
    for repeat in range(STEPS):
        layers = jnp.stack([magnet[..., 0], magnet[..., GX - 1]], axis=1)

        def advance(inputs):
            block_cells, inv_x, inv_y, rate_row, partner_row, side_row, orient_row, offset_row = inputs
            ghosts = []
            for which in range(2):
                source = layers[partner_row[which], side_row[which]]
                mirrored = jnp.where(orient_row[which] == 1, GY - 1 - rows_y, rows_y)
                take_at = ((mirrored + offset_row[which] * ROWS) % GY).astype(jnp.int32)
                ghosts.append(jnp.take(source, take_at, axis=-1).astype(jnp.float32))
            interior = jnp.einsum('fax,fzyx->fzya', inv_x.astype(jnp.float32), block_cells.astype(jnp.float32))
            first_col = inv_x[:, :, 0].astype(jnp.float32)
            last_col = inv_x[:, :, GX - 1].astype(jnp.float32)
            swept_x = interior + first_col[:, None, None, :] * ghosts[0][..., None] + last_col[:, None, None, :] * ghosts[1][..., None]
            swept_x = lax.optimization_barrier(swept_x.astype(jnp.bfloat16))
            swept_y = jnp.einsum('fcy,fzyx->fzcx', inv_y.astype(jnp.float32), swept_x.astype(jnp.float32))
            proton = swept_y[0]
            carbon = swept_y[1]
            new_proton = proton - (rate_row[0] * proton + rate_row[2] * carbon)
            new_carbon = carbon - (rate_row[1] * carbon + rate_row[2] * proton)
            return jnp.stack([new_proton, new_carbon]).astype(jnp.bfloat16)

        magnet = lax.map(advance, (magnet, inverse_x, inverse_y, rates, partner, face_side, orient, offset))
    return magnet
```

```python
import jax
import jax.numpy as jnp
from jax import lax
from jax.sharding import PartitionSpec as P

STEPS = 2


def plane_ghosts(layers, partner_row, side_row, orient_row, offset_row, tile_rows):
    copies = jnp.broadcast_to(layers[None], (lax.axis_size("blk"),) + layers.shape)
    blocks = lax.all_to_all(copies, "blk", split_axis=0, concat_axis=0, tiled=True)
    lines = layers.shape[-1]
    rows_y = jnp.arange(lines, dtype=jnp.int32)
    result = []
    for which in range(2):
        piece = lax.dynamic_index_in_dim(blocks, partner_row[which], 0, keepdims=False)
        segment = lax.dynamic_index_in_dim(piece, side_row[which], 0, keepdims=False)
        mirrored = jnp.where(orient_row[which] == 1, lines - 1 - rows_y, rows_y)
        take_at = (mirrored + offset_row[which] * tile_rows) % lines
        result.append(jnp.take(segment, take_at, axis=-1))
    return result


def local(state, inverse_x, inverse_y, rates, partner, face_side, orient, offset):
    magnet = state[0]
    inv_x = inverse_x[0]
    inv_y = inverse_y[0]
    rate_row = rates[0]
    first_col = inv_x[:, :, 0].astype(jnp.float32)
    last_col = inv_x[:, :, -1].astype(jnp.float32)
    tile_rows = magnet.shape[2]
    planes = lax.all_to_all(magnet, "pen", split_axis=1, concat_axis=2, tiled=True)
    for repeat in range(STEPS):
        layers = jnp.stack([planes[..., 0], planes[..., -1]], axis=0)
        ghosts = plane_ghosts(layers, partner[0], face_side[0], orient[0], offset[0], tile_rows)
        interior = jnp.einsum("fax,fzyx->fzya", inv_x, planes, preferred_element_type=jnp.float32)
        edges = first_col[:, None, None, :] * ghosts[0].astype(jnp.float32)[..., None]
        edges = edges + last_col[:, None, None, :] * ghosts[1].astype(jnp.float32)[..., None]
        swept_x = (interior + edges).astype(jnp.bfloat16)
        swept_y = jnp.einsum("fcy,fzyx->fzcx", inv_y, swept_x, preferred_element_type=jnp.float32)
        proton = swept_y[0]
        carbon = swept_y[1]
        new_proton = proton - (rate_row[0] * proton + rate_row[2] * carbon)
        new_carbon = carbon - (rate_row[1] * carbon + rate_row[2] * proton)
        planes = jnp.stack([new_proton, new_carbon]).astype(jnp.bfloat16)
    magnet = lax.all_to_all(planes, "pen", split_axis=2, concat_axis=1, tiled=True)
    return magnet[None]


def solution(mesh):
    return jax.shard_map(
        local,
        mesh=mesh,
        in_specs=(
            P("blk", None, None, "pen", None),
            P("blk", None, None, None),
            P("blk", None, None, None),
            P("blk", None),
            P("blk", None),
            P("blk", None),
            P("blk", None),
            P("blk", None),
        ),
        out_specs=P("blk", None, None, "pen", None),
        check_vma=False,
    )
```

```python
import functools

import jax
import jax.numpy as jnp
from jax import lax
from jax.experimental import pallas as pl
from jax.experimental.pallas import tpu as pltpu
from jax.sharding import PartitionSpec as P

STEPS = 2
SLOT_ROWS = 8
F32 = jnp.float32
BF16 = jnp.bfloat16
VMEM = pl.BlockSpec(memory_space=pltpu.VMEM)
SMEM = pl.BlockSpec(memory_space=pltpu.SMEM)
NT = (((1,), (1,)), ((), ()))
TN = (((0,), (0,)), ((), ()))


def params():
    return pltpu.CompilerParams(vmem_limit_bytes=32 * 1024 * 1024)


def rows_of(shape):
    return lax.broadcasted_iota(jnp.int32, shape, 0)


def transpose_kernel(source, target):
    for field in range(2):
        target[:, field] = source[field]


def untranspose_kernel(source, target):
    for field in range(2):
        target[field] = source[:, field]


def to_planes(state):
    fields, planes, lines, cells = state.shape
    chunk = planes // 4
    return pl.pallas_call(
        transpose_kernel,
        out_shape=jax.ShapeDtypeStruct((planes, fields, lines, cells), BF16),
        grid=(4,),
        in_specs=[pl.BlockSpec((fields, chunk, lines, cells), lambda i: (0, i, 0, 0))],
        out_specs=pl.BlockSpec((chunk, fields, lines, cells), lambda i: (i, 0, 0, 0)),
        name="to_planes",
    )(state)


def from_planes(moved):
    planes, fields, lines, cells = moved.shape
    chunk = planes // 4
    return pl.pallas_call(
        untranspose_kernel,
        out_shape=jax.ShapeDtypeStruct((fields, planes, lines, cells), BF16),
        grid=(4,),
        in_specs=[pl.BlockSpec((chunk, fields, lines, cells), lambda i: (i, 0, 0, 0))],
        out_specs=pl.BlockSpec((fields, chunk, lines, cells), lambda i: (0, i, 0, 0)),
        name="from_planes",
    )(moved)


def field_plane(planes, field):
    cells = planes.shape[-1]
    return planes[:, field].reshape(-1, cells)


def ends_kernel(inv_x, ends):
    cells = inv_x.shape[-1]
    lane = lax.broadcasted_iota(jnp.int32, (16, cells), 1)
    row = rows_of((16, cells))
    pick = ((row == 0) & (lane == 0)) | ((row == 1) & (lane == cells - 1))
    pick = jnp.where(pick, 1.0, 0.0).astype(BF16)
    for field in range(2):
        ends[field] = lax.dot_general(pick, inv_x[field], NT, preferred_element_type=F32).astype(BF16)


def layers_kernel(planes, sent):
    cells = planes.shape[-1]
    total = None
    lane = lax.broadcasted_iota(jnp.int32, (SLOT_ROWS, 128), 1)
    row = rows_of((SLOT_ROWS, 128))
    for field in range(2):
        for end in range(2):
            pick = (row == field * 2 + end) & (lane == end * 127)
            pick = jnp.where(pick, 1.0, 0.0).astype(BF16)
            start = end * (cells - 128)
            edge = planes[:, field, :, start:start + 128].reshape(-1, 128)
            part = lax.dot_general(pick, edge, NT, preferred_element_type=F32)
            total = part if total is None else total + part
    total = total.astype(BF16)
    for slot in range(sent.shape[0]):
        sent[slot] = total


def interior_kernel(planes, inv_x, interior, corners):
    cells = inv_x.shape[-1]
    row = rows_of((16, cells))
    for field in range(2):
        plane = field_plane(planes, field)
        weights = inv_x[field]
        interior[field] = lax.dot_general(plane, weights, NT, preferred_element_type=F32)
        first = weights[0:16].astype(F32)[0:1]
        last = weights[cells - 16:cells].astype(F32)[15:16]
        two = jnp.where(row == 0, first, jnp.where(row == 1, last, 0.0)).astype(BF16)
        corners[field] = lax.dot_general(two, plane, NT, preferred_element_type=F32)[0:8]


def turned(layer, orient, shift):
    cells = layer.shape[-1]
    layer = pltpu.roll(layer, lax.rem(cells - shift, cells), 1)
    back = 127 - lax.broadcasted_iota(jnp.int32, (layer.shape[0], 128), 1)
    pieces = [
        jnp.take_along_axis(layer[:, at:at + 128], back, axis=1)
        for at in range(cells - 128, -1, -128)
    ]
    return jnp.where(orient == 1, jnp.concatenate(pieces, axis=1), layer)


def ghost_rows(tables, blocks, tile_rows):
    result = []
    for which in range(2):
        layer = blocks[tables[0, which]].astype(F32)
        moved = pltpu.roll(layer, SLOT_ROWS - 1, 0)
        layer = jnp.where(tables[1, which] == 1, moved, layer)
        result.append(turned(layer, tables[2, which], tables[3, which] * tile_rows))
    return result


def packed_ghosts(sides, field):
    cells = sides[0].shape[-1]
    row = rows_of((16, cells))
    at = field * 2
    low = sides[0][at:at + 1]
    high = sides[1][at:at + 1]
    return jnp.where(row == 0, low, jnp.where(row == 1, high, 0.0)).astype(BF16)


def mix(rates, proton, carbon):
    new_proton = proton - (rates[0, 0] * proton + rates[0, 2] * carbon)
    new_carbon = carbon - (rates[0, 1] * carbon + rates[0, 2] * proton)
    return new_proton, new_carbon


def next_layers_kernel(tile_rows, tables, rates, blocks, corners, ends, inv_y, sent, ghosts):
    cells = ends.shape[-1]
    sides = ghost_rows(tables, blocks, tile_rows)
    row = rows_of((16, cells))
    swept = []
    for field in range(2):
        at = field * 2
        edge = ends[field].astype(F32)
        ghosts[field] = packed_ghosts(sides, field)
        found = []
        for end in range(2):
            lane = end * (cells - 1)
            value = corners[field][end:end + 1]
            for which in range(2):
                value = value + edge[which:which + 1, lane:lane + 1] * sides[which][at:at + 1]
            found.append(value)
        two = jnp.where(row == 0, found[0], jnp.where(row == 1, found[1], 0.0)).astype(BF16)
        swept.append(lax.dot_general(two, inv_y[field], NT, preferred_element_type=F32)[0:8])
    new_proton, new_carbon = mix(rates, swept[0], swept[1])
    row8 = rows_of(new_proton.shape)
    total = jnp.where(row8 < 2, new_proton, pltpu.roll(new_carbon, 2, 0)).astype(BF16)
    for slot in range(sent.shape[0]):
        sent[slot] = total


def second_sweep(rates, interior, ghosts, ends, inv_y, emit):
    lines = inv_y.shape[-2]
    swept = []
    for field in range(2):
        outer = lax.dot_general(ghosts[field], ends[field], TN, preferred_element_type=F32)
        swept.append((interior[field] + outer).astype(BF16))
    chunk = lines // 2
    for start in range(0, lines, chunk):
        moved = [
            jnp.dot(inv_y[field, start:start + chunk], swept[field], preferred_element_type=F32)
            for field in range(2)
        ]
        new = mix(rates, moved[0], moved[1])
        for field in range(2):
            emit(field, start, chunk, new[field].astype(BF16))


def middle_kernel(rates, interior, ghosts, ends, inv_y, inv_x, following):
    def emit(field, start, chunk, values):
        following[field, start:start + chunk] = lax.dot_general(
            values, inv_x[field], NT, preferred_element_type=F32
        )

    second_sweep(rates, interior, ghosts, ends, inv_y, emit)


def last_kernel(tile_rows, tables, rates, blocks, interior, ends, inv_y, planes):
    sides = ghost_rows(tables, blocks, tile_rows)
    ghosts = [packed_ghosts(sides, field) for field in range(2)]
    cells = ends.shape[-1]

    def emit(field, start, chunk, values):
        first = start // tile_rows
        planes[first:first + chunk // tile_rows, field] = values.reshape(-1, tile_rows, cells)

    second_sweep(rates, interior, ghosts, ends, inv_y, emit)


def cost(flops, nbytes):
    return pl.CostEstimate(flops=flops, bytes_accessed=nbytes, transcendentals=0)


def local(state, inverse_x, inverse_y, rates, partner, face_side, orient, offset):
    magnet = state[0]
    inv_x = inverse_x[0]
    inv_y = inverse_y[0]
    fields, depth, tile_rows, cells = magnet.shape
    lines = inv_y.shape[-1]
    count = lax.axis_size("blk")
    tables = jnp.concatenate([partner, face_side, orient, offset], axis=0)
    slots = jax.ShapeDtypeStruct((count, SLOT_ROWS, lines), BF16)
    packed = jax.ShapeDtypeStruct((fields, 16, lines), BF16)
    swept = jax.ShapeDtypeStruct((fields, lines, cells), F32)
    sweep_flops = 2 * fields * lines * cells * cells
    array_bytes = 2 * fields * lines * cells

    moved = lax.all_to_all(to_planes(magnet), "pen", split_axis=0, concat_axis=0, tiled=True)
    ends = pl.pallas_call(
        ends_kernel,
        out_shape=jax.ShapeDtypeStruct((fields, 16, cells), BF16),
        in_specs=[VMEM],
        out_specs=VMEM,
        compiler_params=params(),
        cost_estimate=cost(sweep_flops // 16, array_bytes),
        name="ends",
    )(inv_x)
    sent = pl.pallas_call(
        layers_kernel,
        out_shape=slots,
        in_specs=[VMEM],
        out_specs=VMEM,
        compiler_params=params(),
        cost_estimate=cost(sweep_flops // 16, array_bytes),
        name="layers",
    )(moved)
    blocks = lax.all_to_all(sent, "blk", split_axis=0, concat_axis=0, tiled=True)
    interior, corners = pl.pallas_call(
        interior_kernel,
        out_shape=(swept, jax.ShapeDtypeStruct((fields, 8, lines), F32)),
        in_specs=[VMEM, VMEM],
        out_specs=(VMEM, VMEM),
        compiler_params=params(),
        cost_estimate=cost(sweep_flops, 4 * array_bytes),
        name="interior",
    )(moved, inv_x)
    sent, ghosts = pl.pallas_call(
        functools.partial(next_layers_kernel, tile_rows),
        out_shape=(slots, packed),
        in_specs=[SMEM, SMEM, VMEM, VMEM, VMEM, VMEM],
        out_specs=(VMEM, VMEM),
        compiler_params=params(),
        cost_estimate=cost(sweep_flops // 16, array_bytes),
        name="next_layers",
    )(tables, rates, blocks, corners, ends, inv_y)
    blocks = lax.all_to_all(sent, "blk", split_axis=0, concat_axis=0, tiled=True)
    interior = pl.pallas_call(
        middle_kernel,
        out_shape=swept,
        in_specs=[SMEM, VMEM, VMEM, VMEM, VMEM, VMEM],
        out_specs=VMEM,
        compiler_params=params(),
        cost_estimate=cost(2 * sweep_flops, 6 * array_bytes),
        name="middle",
    )(rates, interior, ghosts, ends, inv_y, inv_x)
    planes = pl.pallas_call(
        functools.partial(last_kernel, tile_rows),
        out_shape=jax.ShapeDtypeStruct((lines // tile_rows, fields, tile_rows, cells), BF16),
        in_specs=[SMEM, SMEM, VMEM, VMEM, VMEM, VMEM],
        out_specs=VMEM,
        compiler_params=params(),
        cost_estimate=cost(sweep_flops, 4 * array_bytes),
        name="last",
    )(tables, rates, blocks, interior, ends, inv_y)
    back = lax.all_to_all(planes, "pen", split_axis=0, concat_axis=0, tiled=True)
    return from_planes(back)[None]


def solution(mesh):
    return jax.shard_map(
        local,
        mesh=mesh,
        in_specs=(
            P("blk", None, None, "pen", None),
            P("blk", None, None, None),
            P("blk", None, None, None),
            P("blk", None),
            P("blk", None),
            P("blk", None),
            P("blk", None),
            P("blk", None),
        ),
        out_specs=P("blk", None, None, "pen", None),
        check_vma=False,
    )
```

```python
import functools

import jax
import jax.numpy as jnp
from jax import lax
from jax.experimental import pallas as pl
from jax.experimental.pallas import tpu as pltpu
from jax.sharding import PartitionSpec as P

STEPS = 2
SLOT_ROWS = 8
F32 = jnp.float32
BF16 = jnp.bfloat16
VMEM = pl.BlockSpec(memory_space=pltpu.VMEM)
SMEM = pl.BlockSpec(memory_space=pltpu.SMEM)
NT = (((1,), (1,)), ((), ()))
TN = (((0,), (0,)), ((), ()))


def turned_group(size, first):
    return [[(first + member) % size for member in range(size)]]


def params():
    return pltpu.CompilerParams(vmem_limit_bytes=32 * 1024 * 1024)


def rows_of(shape):
    return lax.broadcasted_iota(jnp.int32, shape, 0)


def transpose_kernel(source, target):
    for field in range(2):
        target[:, field] = source[field]


def untranspose_kernel(source, target):
    for field in range(2):
        target[field] = source[:, field]


def to_planes(state):
    fields, planes, lines, cells = state.shape
    chunk = planes // 4
    return pl.pallas_call(
        transpose_kernel,
        out_shape=jax.ShapeDtypeStruct((planes, fields, lines, cells), BF16),
        grid=(4,),
        in_specs=[pl.BlockSpec((fields, chunk, lines, cells), lambda i: (0, i, 0, 0))],
        out_specs=pl.BlockSpec((chunk, fields, lines, cells), lambda i: (i, 0, 0, 0)),
        name="to_planes",
    )(state)


def from_planes(moved):
    planes, fields, lines, cells = moved.shape
    chunk = planes // 4
    return pl.pallas_call(
        untranspose_kernel,
        out_shape=jax.ShapeDtypeStruct((fields, planes, lines, cells), BF16),
        grid=(4,),
        in_specs=[pl.BlockSpec((chunk, fields, lines, cells), lambda i: (i, 0, 0, 0))],
        out_specs=pl.BlockSpec((fields, chunk, lines, cells), lambda i: (0, i, 0, 0)),
        name="from_planes",
    )(moved)


def in_order(tiles, first):
    count = tiles.shape[0]
    ordered = jnp.concatenate([tiles[count - first:], tiles[:count - first]], axis=0)
    return ordered.reshape(-1, tiles.shape[-1])


def ends_kernel(inv_x, ends):
    cells = inv_x.shape[-1]
    lane = lax.broadcasted_iota(jnp.int32, (16, cells), 1)
    row = rows_of((16, cells))
    pick = ((row == 0) & (lane == 0)) | ((row == 1) & (lane == cells - 1))
    pick = jnp.where(pick, 1.0, 0.0).astype(BF16)
    for field in range(2):
        ends[field] = lax.dot_general(pick, inv_x[field], NT, preferred_element_type=F32).astype(BF16)


def layers_kernel(first, planes, sent):
    cells = planes.shape[-1]
    total = None
    lane = lax.broadcasted_iota(jnp.int32, (SLOT_ROWS, 128), 1)
    row = rows_of((SLOT_ROWS, 128))
    for field in range(2):
        for end in range(2):
            pick = (row == field * 2 + end) & (lane == end * 127)
            pick = jnp.where(pick, 1.0, 0.0).astype(BF16)
            start = end * (cells - 128)
            edge = in_order(planes[:, field, :, start:start + 128], first)
            part = lax.dot_general(pick, edge, NT, preferred_element_type=F32)
            total = part if total is None else total + part
    total = total.astype(BF16)
    for slot in range(sent.shape[0]):
        sent[slot] = total


def interior_kernel(tile0, planes, inv_x, interior, corners):
    cells = inv_x.shape[-1]
    row = rows_of((16, cells))
    for field in range(2):
        plane = in_order(planes[:, field], tile0)
        weights = inv_x[field]
        interior[field] = lax.dot_general(plane, weights, NT, preferred_element_type=F32)
        first = weights[0:16].astype(F32)[0:1]
        last = weights[cells - 16:cells].astype(F32)[15:16]
        two = jnp.where(row == 0, first, jnp.where(row == 1, last, 0.0)).astype(BF16)
        corners[field] = lax.dot_general(two, plane, NT, preferred_element_type=F32)[0:8]


def turned(layer, orient, shift):
    cells = layer.shape[-1]
    layer = pltpu.roll(layer, lax.rem(cells - shift, cells), 1)
    back = 127 - lax.broadcasted_iota(jnp.int32, (layer.shape[0], 128), 1)
    pieces = [
        jnp.take_along_axis(layer[:, at:at + 128], back, axis=1)
        for at in range(cells - 128, -1, -128)
    ]
    return jnp.where(orient == 1, jnp.concatenate(pieces, axis=1), layer)


def ghost_rows(tables, blocks, tile_rows):
    result = []
    count = blocks.shape[0]
    for which in range(2):
        place = lax.rem(tables[0, which] + (count - count // 2), count)
        layer = blocks[place].astype(F32)
        moved = pltpu.roll(layer, SLOT_ROWS - 1, 0)
        layer = jnp.where(tables[1, which] == 1, moved, layer)
        result.append(turned(layer, tables[2, which], tables[3, which] * tile_rows))
    return result


def packed_ghosts(sides, field):
    cells = sides[0].shape[-1]
    row = rows_of((16, cells))
    at = field * 2
    low = sides[0][at:at + 1]
    high = sides[1][at:at + 1]
    return jnp.where(row == 0, low, jnp.where(row == 1, high, 0.0)).astype(BF16)


def mix(rates, proton, carbon):
    new_proton = proton - (rates[0, 0] * proton + rates[0, 2] * carbon)
    new_carbon = carbon - (rates[0, 1] * carbon + rates[0, 2] * proton)
    return new_proton, new_carbon


def next_layers_kernel(tile_rows, tables, rates, blocks, corners, ends, inv_y, sent, ghosts):
    cells = ends.shape[-1]
    sides = ghost_rows(tables, blocks, tile_rows)
    row = rows_of((16, cells))
    swept = []
    for field in range(2):
        at = field * 2
        edge = ends[field].astype(F32)
        ghosts[field] = packed_ghosts(sides, field)
        found = []
        for end in range(2):
            lane = end * (cells - 1)
            value = corners[field][end:end + 1]
            for which in range(2):
                value = value + edge[which:which + 1, lane:lane + 1] * sides[which][at:at + 1]
            found.append(value)
        two = jnp.where(row == 0, found[0], jnp.where(row == 1, found[1], 0.0)).astype(BF16)
        swept.append(lax.dot_general(two, inv_y[field], NT, preferred_element_type=F32)[0:8])
    new_proton, new_carbon = mix(rates, swept[0], swept[1])
    row8 = rows_of(new_proton.shape)
    total = jnp.where(row8 < 2, new_proton, pltpu.roll(new_carbon, 2, 0)).astype(BF16)
    for slot in range(sent.shape[0]):
        sent[slot] = total


def second_sweep(rates, interior, ghosts, ends, inv_y, emit):
    lines = inv_y.shape[-2]
    swept = []
    for field in range(2):
        outer = lax.dot_general(ghosts[field], ends[field], TN, preferred_element_type=F32)
        swept.append((interior[field] + outer).astype(BF16))
    chunk = lines // 2
    for start in range(0, lines, chunk):
        moved = [
            jnp.dot(inv_y[field, start:start + chunk], swept[field], preferred_element_type=F32)
            for field in range(2)
        ]
        new = mix(rates, moved[0], moved[1])
        for field in range(2):
            emit(field, start, chunk, new[field].astype(BF16))


def middle_kernel(rates, interior, ghosts, ends, inv_y, inv_x, following):
    def emit(field, start, chunk, values):
        following[field, start:start + chunk] = lax.dot_general(
            values, inv_x[field], NT, preferred_element_type=F32
        )

    second_sweep(rates, interior, ghosts, ends, inv_y, emit)


def last_kernel(tile_rows, tile0, tables, rates, blocks, interior, ends, inv_y, planes):
    sides = ghost_rows(tables, blocks, tile_rows)
    ghosts = [packed_ghosts(sides, field) for field in range(2)]
    cells = ends.shape[-1]

    def emit(field, start, chunk, values):
        count = planes.shape[0]
        for row in range(0, chunk, tile_rows):
            place = ((start + row) // tile_rows + count - tile0) % count
            planes[place, field] = values[row:row + tile_rows]

    second_sweep(rates, interior, ghosts, ends, inv_y, emit)


def cost(flops, nbytes):
    return pl.CostEstimate(flops=flops, bytes_accessed=nbytes, transcendentals=0)


def local(state, inverse_x, inverse_y, rates, partner, face_side, orient, offset):
    magnet = state[0]
    inv_x = inverse_x[0]
    inv_y = inverse_y[0]
    fields, depth, tile_rows, cells = magnet.shape
    lines = inv_y.shape[-1]
    count = lax.axis_size("blk")
    width = lax.axis_size("pen")
    tile0 = (width * 5) // 8
    across = turned_group(count, count // 2)
    within = turned_group(width, tile0)
    tables = jnp.concatenate([partner, face_side, orient, offset], axis=0)
    slots = jax.ShapeDtypeStruct((count, SLOT_ROWS, lines), BF16)
    packed = jax.ShapeDtypeStruct((fields, 16, lines), BF16)
    swept = jax.ShapeDtypeStruct((fields, lines, cells), F32)
    sweep_flops = 2 * fields * lines * cells * cells
    array_bytes = 2 * fields * lines * cells

    moved = lax.all_to_all(to_planes(magnet), "pen", split_axis=0, concat_axis=0, tiled=True, axis_index_groups=within)
    ends = pl.pallas_call(
        ends_kernel,
        out_shape=jax.ShapeDtypeStruct((fields, 16, cells), BF16),
        in_specs=[VMEM],
        out_specs=VMEM,
        compiler_params=params(),
        cost_estimate=cost(sweep_flops // 16, array_bytes),
        name="ends",
    )(inv_x)
    sent = pl.pallas_call(
        functools.partial(layers_kernel, tile0),
        out_shape=slots,
        in_specs=[VMEM],
        out_specs=VMEM,
        compiler_params=params(),
        cost_estimate=cost(sweep_flops // 16, array_bytes),
        name="layers",
    )(moved)
    blocks = lax.all_to_all(sent, "blk", split_axis=0, concat_axis=0, tiled=True, axis_index_groups=across)
    interior, corners = pl.pallas_call(
        functools.partial(interior_kernel, tile0),
        out_shape=(swept, jax.ShapeDtypeStruct((fields, 8, lines), F32)),
        in_specs=[VMEM, VMEM],
        out_specs=(VMEM, VMEM),
        compiler_params=params(),
        cost_estimate=cost(sweep_flops, 4 * array_bytes),
        name="interior",
    )(moved, inv_x)
    sent, ghosts = pl.pallas_call(
        functools.partial(next_layers_kernel, tile_rows),
        out_shape=(slots, packed),
        in_specs=[SMEM, SMEM, VMEM, VMEM, VMEM, VMEM],
        out_specs=(VMEM, VMEM),
        compiler_params=params(),
        cost_estimate=cost(sweep_flops // 16, array_bytes),
        name="next_layers",
    )(tables, rates, blocks, corners, ends, inv_y)
    blocks = lax.all_to_all(sent, "blk", split_axis=0, concat_axis=0, tiled=True, axis_index_groups=across)
    interior = pl.pallas_call(
        middle_kernel,
        out_shape=swept,
        in_specs=[SMEM, VMEM, VMEM, VMEM, VMEM, VMEM],
        out_specs=VMEM,
        compiler_params=params(),
        cost_estimate=cost(2 * sweep_flops, 6 * array_bytes),
        name="middle",
    )(rates, interior, ghosts, ends, inv_y, inv_x)
    planes = pl.pallas_call(
        functools.partial(last_kernel, tile_rows, tile0),
        out_shape=jax.ShapeDtypeStruct((lines // tile_rows, fields, tile_rows, cells), BF16),
        in_specs=[SMEM, SMEM, VMEM, VMEM, VMEM, VMEM],
        out_specs=VMEM,
        compiler_params=params(),
        cost_estimate=cost(sweep_flops, 4 * array_bytes),
        name="last",
    )(tables, rates, blocks, interior, ends, inv_y)
    back = lax.all_to_all(planes, "pen", split_axis=0, concat_axis=0, tiled=True, axis_index_groups=within)
    return from_planes(back)[None]


def solution(mesh):
    return jax.shard_map(
        local,
        mesh=mesh,
        in_specs=(
            P("blk", None, None, "pen", None),
            P("blk", None, None, None),
            P("blk", None, None, None),
            P("blk", None),
            P("blk", None),
            P("blk", None),
            P("blk", None),
            P("blk", None),
        ),
        out_specs=P("blk", None, None, "pen", None),
        check_vma=False,
    )
```

```python
import functools

import jax
import jax.numpy as jnp
from jax import lax
from jax.experimental import pallas as pl
from jax.experimental.pallas import tpu as pltpu
from jax.sharding import PartitionSpec as P

STEPS = 2
SLOT_ROWS = 4
F32 = jnp.float32
BF16 = jnp.bfloat16
VMEM = pl.BlockSpec(memory_space=pltpu.VMEM)
HBM = pl.BlockSpec(memory_space=pltpu.HBM)
SMEM = pl.BlockSpec(memory_space=pltpu.SMEM)
NT = (((1,), (1,)), ((), ()))
TN = (((0,), (0,)), ((), ()))


def turned_group(size, first):
    return [[(first + member) % size for member in range(size)]]


def params():
    return pltpu.CompilerParams(vmem_limit_bytes=16 * 1024 * 1024)


def rows_of(shape):
    return lax.broadcasted_iota(jnp.int32, shape, 0)


def transfer(pairs, sems):
    copies = [
        pltpu.make_async_copy(source, target, sems.at[number])
        for number, (source, target) in enumerate(pairs)
    ]
    for copy in copies:
        copy.start()
    for copy in copies:
        copy.wait()


def pieces_of(by_field, by_plane, parts):
    chunk = by_plane.shape[0] // parts
    return [
        (by_field.at[field, pl.ds(part * chunk, chunk)], by_plane.at[pl.ds(part * chunk, chunk), field])
        for part in range(parts)
        for field in range(2)
    ]


def to_planes_kernel(source, target, sems):
    transfer(pieces_of(source, target, 4), sems)


def from_planes_kernel(source, target, sems):
    transfer([(held, sent) for sent, held in pieces_of(target, source, 4)], sems)


def to_planes(state):
    fields, planes, lines, cells = state.shape
    return pl.pallas_call(
        to_planes_kernel,
        out_shape=jax.ShapeDtypeStruct((planes, fields, lines, cells), BF16),
        in_specs=[HBM],
        out_specs=VMEM,
        scratch_shapes=[pltpu.SemaphoreType.DMA((8,))],
        compiler_params=params(),
        name="to_planes",
    )(state)


def from_planes(moved):
    planes, fields, lines, cells = moved.shape
    return pl.pallas_call(
        from_planes_kernel,
        out_shape=jax.ShapeDtypeStruct((fields, planes, lines, cells), BF16),
        in_specs=[VMEM],
        out_specs=HBM,
        scratch_shapes=[pltpu.SemaphoreType.DMA((8,))],
        compiler_params=params(),
        name="from_planes",
    )(moved)


def in_order(tiles, first):
    count = tiles.shape[0]
    ordered = jnp.concatenate([tiles[count - first:], tiles[:count - first]], axis=0)
    return ordered.reshape(-1, tiles.shape[-1])


def ends_kernel(inv_x, ends):
    cells = inv_x.shape[-1]
    lane = lax.broadcasted_iota(jnp.int32, (16, cells), 1)
    row = rows_of((16, cells))
    pick = ((row == 0) & (lane == 0)) | ((row == 1) & (lane == cells - 1))
    pick = jnp.where(pick, 1.0, 0.0).astype(BF16)
    for field in range(2):
        ends[field] = lax.dot_general(pick, inv_x[field], NT, preferred_element_type=F32).astype(BF16)


def layers_kernel(first, planes, sent):
    cells = planes.shape[-1]
    total = None
    lane = lax.broadcasted_iota(jnp.int32, (16, 128), 1)
    row = rows_of((16, 128))
    for field in range(2):
        for end in range(2):
            pick = (row == field * 2 + end) & (lane == end * 127)
            pick = jnp.where(pick, 1.0, 0.0).astype(BF16)
            start = end * (cells - 128)
            edge = in_order(planes[:, field, :, start:start + 128], first)
            part = lax.dot_general(pick, edge, NT, preferred_element_type=F32)
            total = part if total is None else total + part
    total = total[0:SLOT_ROWS].astype(BF16)
    for slot in range(sent.shape[0]):
        sent[slot] = total


def interior_kernel(tile0, planes, inv_x, interior, corners):
    cells = inv_x.shape[-1]
    row = rows_of((16, cells))
    for field in range(2):
        plane = in_order(planes[:, field], tile0)
        weights = inv_x[field]
        interior[field] = lax.dot_general(plane, weights, NT, preferred_element_type=F32).astype(BF16)
        first = weights[0:16].astype(F32)[0:1]
        last = weights[cells - 16:cells].astype(F32)[15:16]
        two = jnp.where(row == 0, first, jnp.where(row == 1, last, 0.0)).astype(BF16)
        corners[field] = lax.dot_general(two, plane, NT, preferred_element_type=F32)[0:8]


def turned(layer, orient, shift):
    cells = layer.shape[-1]
    layer = pltpu.roll(layer, lax.rem(cells - shift, cells), 1)
    back = 127 - lax.broadcasted_iota(jnp.int32, (layer.shape[0], 128), 1)
    pieces = [
        jnp.take_along_axis(layer[:, at:at + 128], back, axis=1)
        for at in range(cells - 128, -1, -128)
    ]
    return jnp.where(orient == 1, jnp.concatenate(pieces, axis=1), layer)


def ghost_rows(tables, blocks, origin, tile_rows):
    result = []
    count, _, lines = blocks.shape
    row = rows_of((8, lines))
    for which in range(2):
        place = lax.rem(tables[0, which] + (count - origin), count)
        layer = blocks[place].astype(F32)
        far = tables[1, which] == 1
        proton = jnp.where(far, layer[1:2], layer[0:1])
        carbon = jnp.where(far, layer[3:4], layer[2:3])
        both = jnp.where(row == 0, proton, carbon)
        result.append(turned(both, tables[2, which], tables[3, which] * tile_rows))
    return result


def packed_ghosts(sides, field):
    cells = sides[0].shape[-1]
    row = rows_of((16, cells))
    low = sides[0][field:field + 1]
    high = sides[1][field:field + 1]
    return jnp.where(row == 0, low, jnp.where(row == 1, high, 0.0)).astype(BF16)


def mix(rates, proton, carbon):
    new_proton = proton - (rates[0, 0] * proton + rates[0, 2] * carbon)
    new_carbon = carbon - (rates[0, 1] * carbon + rates[0, 2] * proton)
    return new_proton, new_carbon


def next_layers_kernel(tile_rows, origin, tables, rates, blocks, corners, ends, inv_y, sent, ghosts):
    cells = ends.shape[-1]
    sides = ghost_rows(tables, blocks, origin, tile_rows)
    row = rows_of((16, cells))
    swept = []
    for field in range(2):
        edge = ends[field].astype(F32)
        ghosts[field] = packed_ghosts(sides, field)
        found = []
        for end in range(2):
            lane = end * (cells - 1)
            value = corners[field][end:end + 1]
            for which in range(2):
                value = value + edge[which:which + 1, lane:lane + 1] * sides[which][field:field + 1]
            found.append(value)
        two = jnp.where(row == 0, found[0], jnp.where(row == 1, found[1], 0.0)).astype(BF16)
        swept.append(lax.dot_general(two, inv_y[field], NT, preferred_element_type=F32)[0:8])
    new_proton, new_carbon = mix(rates, swept[0], swept[1])
    row8 = rows_of(new_proton.shape)
    total = jnp.where(row8 < 2, new_proton, pltpu.roll(new_carbon, 2, 0))[0:SLOT_ROWS].astype(BF16)
    for slot in range(sent.shape[0]):
        sent[slot] = total


def second_sweep(rates, interior, ghosts, ends, inv_y, emit):
    lines = inv_y.shape[-2]
    swept = []
    for field in range(2):
        outer = lax.dot_general(ghosts[field], ends[field], TN, preferred_element_type=F32)
        swept.append((interior[field].astype(F32) + outer).astype(BF16))
    chunk = lines // 2
    for start in range(0, lines, chunk):
        moved = [
            jnp.dot(inv_y[field, start:start + chunk], swept[field], preferred_element_type=F32)
            for field in range(2)
        ]
        new = mix(rates, moved[0], moved[1])
        for field in range(2):
            emit(field, start, chunk, new[field].astype(BF16))


def middle_kernel(rates, interior, ghosts, ends, inv_y, far_x, following, inv_x, sem):
    fetch = pltpu.make_async_copy(far_x, inv_x, sem)
    fetch.start()

    def emit(field, start, chunk, values):
        if start == 0 and field == 0:
            fetch.wait()
        following[field, start:start + chunk] = lax.dot_general(
            values, inv_x[field], NT, preferred_element_type=F32
        ).astype(BF16)

    second_sweep(rates, interior, ghosts, ends, inv_y, emit)


def last_kernel(tile_rows, tile0, origin, tables, rates, blocks, interior, ends, inv_y, planes):
    sides = ghost_rows(tables, blocks, origin, tile_rows)
    ghosts = [packed_ghosts(sides, field) for field in range(2)]
    cells = ends.shape[-1]

    def emit(field, start, chunk, values):
        count = planes.shape[0]
        for row in range(0, chunk, tile_rows):
            place = ((start + row) // tile_rows + count - tile0) % count
            planes[place, field] = values[row:row + tile_rows]

    second_sweep(rates, interior, ghosts, ends, inv_y, emit)


def cost(flops, nbytes):
    return pl.CostEstimate(flops=flops, bytes_accessed=nbytes, transcendentals=0)


def local(state, inverse_x, inverse_y, rates, partner, face_side, orient, offset):
    magnet = state[0]
    inv_x = inverse_x[0]
    inv_y = inverse_y[0]
    fields, depth, tile_rows, cells = magnet.shape
    lines = inv_y.shape[-1]
    count = lax.axis_size("blk")
    width = lax.axis_size("pen")
    tile0 = (width * 5) // 8
    origin = (count * 5) // 8
    across = turned_group(count, origin)
    within = turned_group(width, tile0)
    tables = jnp.concatenate([partner, face_side, orient, offset], axis=0)
    slots = jax.ShapeDtypeStruct((count, SLOT_ROWS, lines), BF16)
    packed = jax.ShapeDtypeStruct((fields, 16, lines), BF16)
    swept = jax.ShapeDtypeStruct((fields, lines, cells), BF16)
    sweep_flops = 2 * fields * lines * cells * cells
    array_bytes = 2 * fields * lines * cells

    moved = lax.all_to_all(to_planes(magnet), "pen", split_axis=0, concat_axis=0, tiled=True, axis_index_groups=within)
    ends = pl.pallas_call(
        ends_kernel,
        out_shape=jax.ShapeDtypeStruct((fields, 16, cells), BF16),
        in_specs=[VMEM],
        out_specs=VMEM,
        compiler_params=params(),
        cost_estimate=cost(sweep_flops // 16, array_bytes),
        name="ends",
    )(inv_x)
    sent = pl.pallas_call(
        functools.partial(layers_kernel, tile0),
        out_shape=slots,
        in_specs=[VMEM],
        out_specs=VMEM,
        compiler_params=params(),
        cost_estimate=cost(sweep_flops // 16, array_bytes),
        name="layers",
    )(moved)
    blocks = lax.all_to_all(sent, "blk", split_axis=0, concat_axis=0, tiled=True, axis_index_groups=across)
    interior, corners = pl.pallas_call(
        functools.partial(interior_kernel, tile0),
        out_shape=(swept, jax.ShapeDtypeStruct((fields, 8, lines), F32)),
        in_specs=[VMEM, VMEM],
        out_specs=(VMEM, VMEM),
        compiler_params=params(),
        cost_estimate=cost(sweep_flops, 4 * array_bytes),
        name="interior",
    )(moved, inv_x)
    sent, ghosts = pl.pallas_call(
        functools.partial(next_layers_kernel, tile_rows, origin),
        out_shape=(slots, packed),
        in_specs=[SMEM, SMEM, VMEM, VMEM, VMEM, VMEM],
        out_specs=(VMEM, VMEM),
        compiler_params=params(),
        cost_estimate=cost(sweep_flops // 16, array_bytes),
        name="next_layers",
    )(tables, rates, blocks, corners, ends, inv_y)
    blocks = lax.all_to_all(sent, "blk", split_axis=0, concat_axis=0, tiled=True, axis_index_groups=across)
    interior = pl.pallas_call(
        middle_kernel,
        out_shape=swept,
        in_specs=[SMEM, VMEM, VMEM, VMEM, VMEM, HBM],
        out_specs=VMEM,
        scratch_shapes=[pltpu.VMEM(inv_x.shape, BF16), pltpu.SemaphoreType.DMA],
        compiler_params=params(),
        cost_estimate=cost(2 * sweep_flops, 6 * array_bytes),
        name="middle",
    )(rates, interior, ghosts, ends, inv_y, inv_x)
    planes = pl.pallas_call(
        functools.partial(last_kernel, tile_rows, tile0, origin),
        out_shape=jax.ShapeDtypeStruct((lines // tile_rows, fields, tile_rows, cells), BF16),
        in_specs=[SMEM, SMEM, VMEM, VMEM, VMEM, VMEM],
        out_specs=VMEM,
        compiler_params=params(),
        cost_estimate=cost(sweep_flops, 4 * array_bytes),
        name="last",
    )(tables, rates, blocks, interior, ends, inv_y)
    back = lax.all_to_all(planes, "pen", split_axis=0, concat_axis=0, tiled=True, axis_index_groups=within)
    return from_planes(back)[None]


def solution(mesh):
    return jax.shard_map(
        local,
        mesh=mesh,
        in_specs=(
            P("blk", None, None, "pen", None),
            P("blk", None, None, None),
            P("blk", None, None, None),
            P("blk", None),
            P("blk", None),
            P("blk", None),
            P("blk", None),
            P("blk", None),
        ),
        out_specs=P("blk", None, None, "pen", None),
        check_vma=False,
    )
```

```python
import functools

import jax
import jax.numpy as jnp
from jax import lax
from jax.experimental import pallas as pl
from jax.experimental.pallas import tpu as pltpu
from jax.sharding import PartitionSpec as P

STEPS = 2
SLOT_ROWS = 4
F32 = jnp.float32
BF16 = jnp.bfloat16
VMEM = pl.BlockSpec(memory_space=pltpu.VMEM)
HBM = pl.BlockSpec(memory_space=pltpu.HBM)
SMEM = pl.BlockSpec(memory_space=pltpu.SMEM)
NT = (((1,), (1,)), ((), ()))
TN = (((0,), (0,)), ((), ()))


def turned_group(size, first):
    return [[(first + member) % size for member in range(size)]]


def params():
    return pltpu.CompilerParams(vmem_limit_bytes=16 * 1024 * 1024)


def rows_of(shape):
    return lax.broadcasted_iota(jnp.int32, shape, 0)


def transfer(pairs, sems):
    copies = [
        pltpu.make_async_copy(source, target, sems.at[number])
        for number, (source, target) in enumerate(pairs)
    ]
    for copy in copies:
        copy.start()
    for copy in copies:
        copy.wait()


def pieces_of(by_field, by_plane, parts):
    chunk = by_plane.shape[0] // parts
    return [
        (by_field.at[field, pl.ds(part * chunk, chunk)], by_plane.at[pl.ds(part * chunk, chunk), field])
        for part in range(parts)
        for field in range(2)
    ]


def to_planes_kernel(source, target, sems):
    transfer(pieces_of(source, target, 4), sems)


def from_planes_kernel(source, target, sems):
    transfer([(held, sent) for sent, held in pieces_of(target, source, 4)], sems)


def to_planes(state):
    fields, planes, lines, cells = state.shape
    return pl.pallas_call(
        to_planes_kernel,
        out_shape=jax.ShapeDtypeStruct((planes, fields, lines, cells), BF16),
        in_specs=[HBM],
        out_specs=VMEM,
        scratch_shapes=[pltpu.SemaphoreType.DMA((8,))],
        compiler_params=params(),
        name="to_planes",
    )(state)


def from_planes(moved):
    planes, fields, lines, cells = moved.shape
    return pl.pallas_call(
        from_planes_kernel,
        out_shape=jax.ShapeDtypeStruct((fields, planes, lines, cells), BF16),
        in_specs=[VMEM],
        out_specs=HBM,
        scratch_shapes=[pltpu.SemaphoreType.DMA((8,))],
        compiler_params=params(),
        name="from_planes",
    )(moved)


def in_order(tiles, first):
    count = tiles.shape[0]
    ordered = jnp.concatenate([tiles[count - first:], tiles[:count - first]], axis=0)
    return ordered.reshape(-1, tiles.shape[-1])


def table_rows(lines, tile_rows):
    bits = (lines // tile_rows).bit_length() - 1
    names = ["proton", "carbon", "cross"]
    for which in range(2):
        names += [("place", which), ("far", which), ("turn", which)]
        names += [("bit", which, bit) for bit in range(bits)]
    return names


def prepare_kernel(tile_rows, origin, count, tables, rates, inv_x, ends, consts):
    cells = inv_x.shape[-1]
    lane = lax.broadcasted_iota(jnp.int32, (16, cells), 1)
    row = rows_of((16, cells))
    pick = ((row == 0) & (lane == 0)) | ((row == 1) & (lane == cells - 1))
    pick = jnp.where(pick, 1.0, 0.0).astype(BF16)
    for field in range(2):
        ends[field] = lax.dot_general(pick, inv_x[field], NT, preferred_element_type=F32).astype(BF16)
    values = [rates[0, number] for number in range(3)]
    for which in range(2):
        place = lax.rem(tables[0, which] + (count - origin), count)
        numbers = [place, tables[1, which], tables[2, which]]
        bits = len(table_rows(cells, tile_rows)) // 2 - 4
        numbers += [(tables[3, which] >> bit) & 1 for bit in range(bits)]
        values += [number.astype(F32) for number in numbers]
    shape = consts.shape
    at = rows_of(shape)
    filled = jnp.zeros(shape, F32)
    for number, value in enumerate(values):
        filled = jnp.where(at == number, value, filled)
    consts[...] = filled


def layers_kernel(first, planes, sent):
    cells = planes.shape[-1]
    total = None
    lane = lax.broadcasted_iota(jnp.int32, (16, 128), 1)
    row = rows_of((16, 128))
    for field in range(2):
        for end in range(2):
            pick = (row == field * 2 + end) & (lane == end * 127)
            pick = jnp.where(pick, 1.0, 0.0).astype(BF16)
            start = end * (cells - 128)
            edge = in_order(planes[:, field, :, start:start + 128], first)
            part = lax.dot_general(pick, edge, NT, preferred_element_type=F32)
            total = part if total is None else total + part
    total = total[0:SLOT_ROWS].astype(BF16)
    for slot in range(sent.shape[0]):
        sent[slot] = total


def corners_kernel(tile0, planes, inv_x, corners):
    cells = inv_x.shape[-1]
    row = rows_of((16, cells))
    for field in range(2):
        plane = in_order(planes[:, field], tile0)
        first = inv_x[field, 0:16].astype(F32)[0:1]
        last = inv_x[field, cells - 16:cells].astype(F32)[15:16]
        two = jnp.where(row == 0, first, jnp.where(row == 1, last, 0.0)).astype(BF16)
        corners[field] = lax.dot_general(two, plane, NT, preferred_element_type=F32)[0:8]


def constant(consts, names, name, lines):
    at = names.index(name)
    return jnp.concatenate([consts[at:at + 1]] * (lines // consts.shape[1]), axis=1)


def mirrored(layer):
    cells = layer.shape[-1]
    back = 127 - lax.broadcasted_iota(jnp.int32, (layer.shape[0], 128), 1)
    pieces = [
        jnp.take_along_axis(layer[:, at:at + 128], back, axis=1)
        for at in range(cells - 128, -1, -128)
    ]
    return jnp.concatenate(pieces, axis=1)


def ghost_rows(consts, blocks, tile_rows):
    result = []
    count, _, lines = blocks.shape
    names = table_rows(lines, tile_rows)
    row = rows_of((8, lines))
    for which in range(2):
        get = lambda *name: constant(consts, names, name, lines)
        place = get("place", which)
        layer = blocks[0].astype(F32)
        for slot in range(1, count):
            layer = jnp.where(place == slot, blocks[slot].astype(F32), layer)
        far = get("far", which) == 1
        proton = jnp.where(far, layer[1:2], layer[0:1])
        carbon = jnp.where(far, layer[3:4], layer[2:3])
        both = jnp.where(row == 0, proton, carbon)
        for bit in range(len(names) // 2 - 4):
            moved = pltpu.roll(both, lines - (tile_rows << bit), 1)
            both = jnp.where(get("bit", which, bit) == 1, moved, both)
        result.append(jnp.where(get("turn", which) == 1, mirrored(both), both))
    return result


def packed_ghosts(sides, field):
    cells = sides[0].shape[-1]
    row = rows_of((16, cells))
    low = sides[0][field:field + 1]
    high = sides[1][field:field + 1]
    return jnp.where(row == 0, low, jnp.where(row == 1, high, 0.0)).astype(BF16)


def mix(consts, tile_rows, proton, carbon):
    lines = proton.shape[-1]
    names = table_rows(lines, tile_rows)
    first, second, cross = (constant(consts, names, name, lines) for name in names[:3])
    new_proton = proton - (first * proton + cross * carbon)
    new_carbon = carbon - (second * carbon + cross * proton)
    return new_proton, new_carbon


def next_layers_kernel(tile_rows, consts, blocks, corners, ends, inv_y, sent, ghosts):
    cells = ends.shape[-1]
    sides = ghost_rows(consts, blocks, tile_rows)
    row = rows_of((16, cells))
    swept = []
    for field in range(2):
        edge = ends[field].astype(F32)
        ghosts[field] = packed_ghosts(sides, field)
        found = []
        for end in range(2):
            lane = end * (cells - 1)
            value = corners[field][end:end + 1]
            for which in range(2):
                value = value + edge[which:which + 1, lane:lane + 1] * sides[which][field:field + 1]
            found.append(value)
        two = jnp.where(row == 0, found[0], jnp.where(row == 1, found[1], 0.0)).astype(BF16)
        swept.append(lax.dot_general(two, inv_y[field], NT, preferred_element_type=F32)[0:8])
    new_proton, new_carbon = mix(consts, tile_rows, swept[0], swept[1])
    row8 = rows_of(new_proton.shape)
    total = jnp.where(row8 < 2, new_proton, pltpu.roll(new_carbon, 2, 0))[0:SLOT_ROWS].astype(BF16)
    for slot in range(sent.shape[0]):
        sent[slot] = total


def second_sweep(consts, tile_rows, interior, ghosts, ends, inv_y, emit):
    lines = inv_y.shape[-2]
    swept = []
    for field in range(2):
        outer = lax.dot_general(ghosts[field], ends[field], TN, preferred_element_type=F32)
        swept.append((interior(field) + outer).astype(BF16))
    chunk = lines // 2
    for start in range(0, lines, chunk):
        moved = [
            jnp.dot(inv_y[field, start:start + chunk], swept[field], preferred_element_type=F32)
            for field in range(2)
        ]
        new = mix(consts, tile_rows, moved[0], moved[1])
        for field in range(2):
            emit(field, start, chunk, new[field].astype(BF16))


def middle_kernel(tile_rows, tile0, consts, planes, ghosts, ends, inv_y, inv_x, following):
    def interior(field):
        plane = in_order(planes[:, field], tile0)
        return lax.dot_general(plane, inv_x[field], NT, preferred_element_type=F32)

    def emit(field, start, chunk, values):
        rows = lax.dot_general(values, inv_x[field], NT, preferred_element_type=F32)
        rows = rows.astype(BF16).reshape(-1, tile_rows, rows.shape[-1])
        first = start // tile_rows
        following[first:first + rows.shape[0], field] = rows

    second_sweep(consts, tile_rows, interior, ghosts, ends, inv_y, emit)


def last_kernel(tile_rows, tile0, consts, blocks, interior, ends, inv_y, planes):
    sides = ghost_rows(consts, blocks, tile_rows)
    ghosts = [packed_ghosts(sides, field) for field in range(2)]

    def whole(field):
        return interior[:, field].reshape(-1, interior.shape[-1]).astype(F32)

    def emit(field, start, chunk, values):
        count = planes.shape[0]
        for row in range(0, chunk, tile_rows):
            place = ((start + row) // tile_rows + count - tile0) % count
            planes[place, field] = values[row:row + tile_rows]

    second_sweep(
        consts, tile_rows, whole, ghosts, ends, inv_y, emit
    )


def cost(flops, nbytes):
    return pl.CostEstimate(flops=flops, bytes_accessed=nbytes, transcendentals=0)


def local(state, inverse_x, inverse_y, rates, partner, face_side, orient, offset):
    magnet = state[0]
    inv_x = inverse_x[0]
    inv_y = inverse_y[0]
    fields, depth, tile_rows, cells = magnet.shape
    lines = inv_y.shape[-1]
    count = lax.axis_size("blk")
    width = lax.axis_size("pen")
    tile0 = (width * 5) // 8
    origin = (count * 5) // 8
    across = turned_group(count, origin)
    within = turned_group(width, tile0)
    tables = jnp.concatenate([partner, face_side, orient, offset], axis=0)
    slots = jax.ShapeDtypeStruct((count, SLOT_ROWS, lines), BF16)
    packed = jax.ShapeDtypeStruct((fields, 16, lines), BF16)
    sweep_flops = 2 * fields * lines * cells * cells
    array_bytes = 2 * fields * lines * cells

    moved = lax.all_to_all(to_planes(magnet), "pen", split_axis=0, concat_axis=0, tiled=True, axis_index_groups=within)
    ends, consts = pl.pallas_call(
        functools.partial(prepare_kernel, tile_rows, origin, count),
        out_shape=(packed, jax.ShapeDtypeStruct((24, 128), F32)),
        in_specs=[SMEM, SMEM, VMEM],
        out_specs=(VMEM, VMEM),
        compiler_params=params(),
        cost_estimate=cost(sweep_flops // 16, array_bytes),
        name="prepare",
    )(tables, rates, inv_x)
    sent = pl.pallas_call(
        functools.partial(layers_kernel, tile0),
        out_shape=slots,
        in_specs=[VMEM],
        out_specs=VMEM,
        compiler_params=params(),
        cost_estimate=cost(sweep_flops // 16, array_bytes),
        name="layers",
    )(moved)
    blocks = lax.all_to_all(sent, "blk", split_axis=0, concat_axis=0, tiled=True, axis_index_groups=across)
    corners = pl.pallas_call(
        functools.partial(corners_kernel, tile0),
        out_shape=jax.ShapeDtypeStruct((fields, 8, lines), F32),
        in_specs=[VMEM, VMEM],
        out_specs=VMEM,
        compiler_params=params(),
        cost_estimate=cost(sweep_flops // 16, 2 * array_bytes),
        name="corners",
    )(moved, inv_x)
    sent, ghosts = pl.pallas_call(
        functools.partial(next_layers_kernel, tile_rows),
        out_shape=(slots, packed),
        in_specs=[VMEM] * 5,
        out_specs=(VMEM, VMEM),
        compiler_params=params(),
        cost_estimate=cost(sweep_flops // 16, array_bytes),
        name="next_layers",
    )(consts, blocks, corners, ends, inv_y)
    blocks = lax.all_to_all(sent, "blk", split_axis=0, concat_axis=0, tiled=True, axis_index_groups=across)
    interior = pl.pallas_call(
        functools.partial(middle_kernel, tile_rows, tile0),
        out_shape=jax.ShapeDtypeStruct(moved.shape, BF16),
        input_output_aliases={1: 0},
        in_specs=[VMEM] * 6,
        out_specs=VMEM,
        compiler_params=params(),
        cost_estimate=cost(3 * sweep_flops, 4 * array_bytes),
        name="middle",
    )(consts, moved, ghosts, ends, inv_y, inv_x)
    planes = pl.pallas_call(
        functools.partial(last_kernel, tile_rows, tile0),
        out_shape=jax.ShapeDtypeStruct((lines // tile_rows, fields, tile_rows, cells), BF16),
        in_specs=[VMEM] * 5,
        out_specs=VMEM,
        compiler_params=params(),
        cost_estimate=cost(sweep_flops, 4 * array_bytes),
        name="last",
    )(consts, blocks, interior, ends, inv_y)
    back = lax.all_to_all(planes, "pen", split_axis=0, concat_axis=0, tiled=True, axis_index_groups=within)
    return from_planes(back)[None]


def solution(mesh):
    return jax.shard_map(
        local,
        mesh=mesh,
        in_specs=(
            P("blk", None, None, "pen", None),
            P("blk", None, None, None),
            P("blk", None, None, None),
            P("blk", None),
            P("blk", None),
            P("blk", None),
            P("blk", None),
            P("blk", None),
        ),
        out_specs=P("blk", None, None, "pen", None),
        check_vma=False,
    )
```

```python
import functools

import jax
import jax.numpy as jnp
from jax import lax
from jax.experimental import pallas as pl
from jax.experimental.pallas import tpu as pltpu
from jax.sharding import PartitionSpec as P

STEPS = 2
SLOT_ROWS = 4
F32 = jnp.float32
BF16 = jnp.bfloat16
VMEM = pl.BlockSpec(memory_space=pltpu.VMEM)
HBM = pl.BlockSpec(memory_space=pltpu.HBM)
SMEM = pl.BlockSpec(memory_space=pltpu.SMEM)
NT = (((1,), (1,)), ((), ()))
TN = (((0,), (0,)), ((), ()))


def turned_group(size, first):
    return [[(first + member) % size for member in range(size)]]


def params():
    return pltpu.CompilerParams(vmem_limit_bytes=16 * 1024 * 1024)


def rows_of(shape):
    return lax.broadcasted_iota(jnp.int32, shape, 0)


def transfer(pairs, sems):
    copies = [
        pltpu.make_async_copy(source, target, sems.at[number])
        for number, (source, target) in enumerate(pairs)
    ]
    for copy in copies:
        copy.start()
    for copy in copies:
        copy.wait()


def pieces_of(by_field, by_plane, parts):
    chunk = by_plane.shape[0] // parts
    return [
        (by_field.at[field, pl.ds(part * chunk, chunk)], by_plane.at[pl.ds(part * chunk, chunk), field])
        for part in range(parts)
        for field in range(2)
    ]


def to_planes_kernel(source, target, sems):
    transfer(pieces_of(source, target, 1), sems)


def from_planes_kernel(source, target, sems):
    transfer([(held, sent) for sent, held in pieces_of(target, source, 1)], sems)


def to_planes(state):
    fields, planes, lines, cells = state.shape
    return pl.pallas_call(
        to_planes_kernel,
        out_shape=jax.ShapeDtypeStruct((planes, fields, lines, cells), BF16),
        in_specs=[HBM],
        out_specs=VMEM,
        scratch_shapes=[pltpu.SemaphoreType.DMA((2,))],
        compiler_params=pltpu.CompilerParams(vmem_limit_bytes=52 * 1024 * 1024),
        name="to_planes",
    )(state)


def from_planes(moved):
    planes, fields, lines, cells = moved.shape
    return pl.pallas_call(
        from_planes_kernel,
        out_shape=jax.ShapeDtypeStruct((fields, planes, lines, cells), BF16),
        in_specs=[VMEM],
        out_specs=HBM,
        scratch_shapes=[pltpu.SemaphoreType.DMA((2,))],
        compiler_params=params(),
        name="from_planes",
    )(moved)


def in_order(tiles, first):
    count = tiles.shape[0]
    ordered = jnp.concatenate([tiles[count - first:], tiles[:count - first]], axis=0)
    return ordered.reshape(-1, tiles.shape[-1])


def shift_bits(lines, tile_rows):
    return (lines // tile_rows).bit_length() - 1


def constant_names(lines, tile_rows):
    return ["proton", "carbon", "cross", "place", "far", "turn", *range(shift_bits(lines, tile_rows))]


def prepare_kernel(tile_rows, origin, count, tables, rates, inv_x, ends, consts):
    cells = inv_x.shape[-1]
    lane = lax.broadcasted_iota(jnp.int32, (16, cells), 1)
    row = rows_of((16, cells))
    pick = ((row == 0) & (lane == 0)) | ((row == 1) & (lane == cells - 1))
    pick = jnp.where(pick, 1.0, 0.0).astype(BF16)
    for field in range(2):
        ends[field] = lax.dot_general(pick, inv_x[field], NT, preferred_element_type=F32).astype(BF16)
    values = [(rates[0, number], rates[0, number]) for number in range(3)]
    sides = []
    for which in range(2):
        place = lax.rem(tables[0, which] + (count - origin), count)
        numbers = [place, tables[1, which], tables[2, which]]
        numbers += [(tables[3, which] >> bit) & 1 for bit in range(shift_bits(cells, tile_rows))]
        sides.append([number.astype(F32) for number in numbers])
    values += zip(*sides)
    upper = rows_of((8, consts.shape[1])) < 2
    for number, (low, high) in enumerate(values):
        consts[8 * number:8 * number + 8] = jnp.where(upper, low, high)


def layers_kernel(first, planes, sent):
    cells = planes.shape[-1]
    lane = lax.broadcasted_iota(jnp.int32, (16, 512), 1)
    row = rows_of((16, 512))
    pick = (row < SLOT_ROWS) & (lane == row * 128 + jnp.where(row >= 2, 127, 0))
    pick = jnp.where(pick, 1.0, 0.0).astype(BF16)
    edges = [
        in_order(planes[:, field, :, start:start + 128], first)
        for start in (0, cells - 128)
        for field in range(2)
    ]
    total = lax.dot_general(pick, jnp.concatenate(edges, axis=1), NT, preferred_element_type=F32)
    total = total[0:SLOT_ROWS].astype(BF16)
    for slot in range(sent.shape[0]):
        sent[slot] = total


def corners_kernel(tile0, planes, inv_x, corners):
    cells = inv_x.shape[-1]
    row = rows_of((16, cells))
    for field in range(2):
        plane = in_order(planes[:, field], tile0)
        first = inv_x[field, 0:16].astype(F32)[0:1]
        last = inv_x[field, cells - 16:cells].astype(F32)[15:16]
        two = jnp.where(row == 0, first, jnp.where(row == 1, last, 0.0)).astype(BF16)
        corners[field] = lax.dot_general(two, plane, NT, preferred_element_type=F32)[0:8]


def constant(consts, names, name, lines):
    at = 8 * names.index(name)
    return jnp.concatenate([consts[at:at + 8]] * (lines // consts.shape[1]), axis=1)


def mirrored(layer):
    cells = layer.shape[-1]
    back = 127 - lax.broadcasted_iota(jnp.int32, (layer.shape[0], 128), 1)
    pieces = [
        jnp.take_along_axis(layer[:, at:at + 128], back, axis=1)
        for at in range(cells - 128, -1, -128)
    ]
    return jnp.concatenate(pieces, axis=1)


def ghost_rows(consts, blocks, tile_rows):
    count, _, lines = blocks.shape
    names = constant_names(lines, tile_rows)
    place = constant(consts, names, "place", lines)
    layers = []
    for which in range(2):
        wanted = place[2 * which:2 * which + 1]
        layer = blocks[0].astype(F32)
        for slot in range(1, count):
            layer = jnp.where(wanted == slot, blocks[slot].astype(F32), layer)
        layers.append(layer)
    near = jnp.concatenate([layers[0][0:2], layers[1][0:2]] * 2, axis=0)
    far = jnp.concatenate([layers[0][2:4], layers[1][2:4]] * 2, axis=0)
    rows = jnp.where(constant(consts, names, "far", lines) == 1, far, near)
    for bit in range(shift_bits(lines, tile_rows)):
        moved = pltpu.roll(rows, lines - (tile_rows << bit), 1)
        rows = jnp.where(constant(consts, names, bit, lines) == 1, moved, rows)
    return jnp.where(constant(consts, names, "turn", lines) == 1, mirrored(rows), rows)


def packed_ghosts(found, field):
    row = rows_of((16, found.shape[-1]))
    low = found[field:field + 1]
    high = found[2 + field:3 + field]
    return jnp.where(row == 0, low, jnp.where(row == 1, high, 0.0)).astype(BF16)


def mix(consts, tile_rows, proton, carbon):
    lines = proton.shape[-1]
    names = constant_names(lines, tile_rows)
    first, second, cross = (constant(consts, names, name, lines)[0:1] for name in names[:3])
    new_proton = proton - (first * proton + cross * carbon)
    new_carbon = carbon - (second * carbon + cross * proton)
    return new_proton, new_carbon


def next_layers_kernel(tile_rows, consts, blocks, corners, ends, inv_y, sent, ghosts):
    cells = ends.shape[-1]
    found = ghost_rows(consts, blocks, tile_rows)
    row = rows_of((16, cells))
    swept = []
    for field in range(2):
        edge = ends[field].astype(F32)
        ghosts[field] = packed_ghosts(found, field)
        layers = []
        for end in range(2):
            lane = end * (cells - 1)
            value = corners[field][end:end + 1]
            for which in range(2):
                at = which * 2 + field
                value = value + edge[which:which + 1, lane:lane + 1] * found[at:at + 1]
            layers.append(value)
        two = jnp.where(row == 0, layers[0], jnp.where(row == 1, layers[1], 0.0)).astype(BF16)
        swept.append(lax.dot_general(two, inv_y[field], NT, preferred_element_type=F32)[0:8])
    new_proton, new_carbon = mix(consts, tile_rows, swept[0], swept[1])
    total = jnp.concatenate(
        [new_proton[0:1], new_carbon[0:1], new_proton[1:2], new_carbon[1:2]], axis=0
    ).astype(BF16)
    for slot in range(sent.shape[0]):
        sent[slot] = total


def second_sweep(consts, tile_rows, interior, ghosts, ends, inv_y, emit):
    lines = inv_y.shape[-2]
    swept = []
    for field in range(2):
        outer = lax.dot_general(ghosts[field], ends[field], TN, preferred_element_type=F32)
        swept.append((interior(field) + outer).astype(BF16))
    chunk = lines // 2
    for start in range(0, lines, chunk):
        moved = [
            jnp.dot(inv_y[field, start:start + chunk], swept[field], preferred_element_type=F32)
            for field in range(2)
        ]
        new = mix(consts, tile_rows, moved[0], moved[1])
        for field in range(2):
            emit(field, start, chunk, new[field].astype(BF16))


def middle_kernel(tile_rows, tile0, consts, planes, ghosts, ends, inv_y, inv_x, following):
    def interior(field):
        plane = in_order(planes[:, field], tile0)
        return lax.dot_general(plane, inv_x[field], NT, preferred_element_type=F32)

    def emit(field, start, chunk, values):
        rows = lax.dot_general(values, inv_x[field], NT, preferred_element_type=F32)
        rows = rows.astype(BF16).reshape(-1, tile_rows, rows.shape[-1])
        first = start // tile_rows
        following[first:first + rows.shape[0], field] = rows

    second_sweep(consts, tile_rows, interior, ghosts, ends, inv_y, emit)


def last_kernel(tile_rows, tile0, consts, blocks, interior, ends, inv_y, planes):
    found = ghost_rows(consts, blocks, tile_rows)
    ghosts = [packed_ghosts(found, field) for field in range(2)]

    def whole(field):
        return interior[:, field].reshape(-1, interior.shape[-1]).astype(F32)

    def emit(field, start, chunk, values):
        count = planes.shape[0]
        for row in range(0, chunk, tile_rows):
            place = ((start + row) // tile_rows + count - tile0) % count
            planes[place, field] = values[row:row + tile_rows]

    second_sweep(
        consts, tile_rows, whole, ghosts, ends, inv_y, emit
    )


def cost(flops, nbytes):
    return pl.CostEstimate(flops=flops, bytes_accessed=nbytes, transcendentals=0)


def local(state, inverse_x, inverse_y, rates, partner, face_side, orient, offset):
    magnet = state[0]
    inv_x = inverse_x[0]
    inv_y = inverse_y[0]
    fields, depth, tile_rows, cells = magnet.shape
    lines = inv_y.shape[-1]
    count = lax.axis_size("blk")
    width = lax.axis_size("pen")
    tile0 = (width * 5) // 8
    origin = (count * 5) // 8
    across = turned_group(count, origin)
    within = turned_group(width, tile0)
    tables = jnp.concatenate([partner, face_side, orient, offset], axis=0)
    slots = jax.ShapeDtypeStruct((count, SLOT_ROWS, lines), BF16)
    packed = jax.ShapeDtypeStruct((fields, 16, lines), BF16)
    sweep_flops = 2 * fields * lines * cells * cells
    array_bytes = 2 * fields * lines * cells

    moved = lax.all_to_all(to_planes(magnet), "pen", split_axis=0, concat_axis=0, tiled=True, axis_index_groups=within)
    ends, consts = pl.pallas_call(
        functools.partial(prepare_kernel, tile_rows, origin, count),
        out_shape=(packed, jax.ShapeDtypeStruct((8 * len(constant_names(lines, tile_rows)), 128), F32)),
        in_specs=[SMEM, SMEM, VMEM],
        out_specs=(VMEM, VMEM),
        compiler_params=params(),
        cost_estimate=cost(sweep_flops // 16, array_bytes),
        name="prepare",
    )(tables, rates, inv_x)
    sent = pl.pallas_call(
        functools.partial(layers_kernel, tile0),
        out_shape=slots,
        in_specs=[VMEM],
        out_specs=VMEM,
        compiler_params=params(),
        cost_estimate=cost(sweep_flops // 16, array_bytes),
        name="layers",
    )(moved)
    blocks = lax.all_to_all(sent, "blk", split_axis=0, concat_axis=0, tiled=True, axis_index_groups=across)
    corners = pl.pallas_call(
        functools.partial(corners_kernel, tile0),
        out_shape=jax.ShapeDtypeStruct((fields, 8, lines), F32),
        in_specs=[VMEM, VMEM],
        out_specs=VMEM,
        compiler_params=params(),
        cost_estimate=cost(sweep_flops // 16, 2 * array_bytes),
        name="corners",
    )(moved, inv_x)
    sent, ghosts = pl.pallas_call(
        functools.partial(next_layers_kernel, tile_rows),
        out_shape=(slots, packed),
        in_specs=[VMEM] * 5,
        out_specs=(VMEM, VMEM),
        compiler_params=params(),
        cost_estimate=cost(sweep_flops // 16, array_bytes),
        name="next_layers",
    )(consts, blocks, corners, ends, inv_y)
    blocks = lax.all_to_all(sent, "blk", split_axis=0, concat_axis=0, tiled=True, axis_index_groups=across)
    interior = pl.pallas_call(
        functools.partial(middle_kernel, tile_rows, tile0),
        out_shape=jax.ShapeDtypeStruct(moved.shape, BF16),
        input_output_aliases={1: 0},
        in_specs=[VMEM] * 6,
        out_specs=VMEM,
        compiler_params=params(),
        cost_estimate=cost(3 * sweep_flops, 4 * array_bytes),
        name="middle",
    )(consts, moved, ghosts, ends, inv_y, inv_x)
    planes = pl.pallas_call(
        functools.partial(last_kernel, tile_rows, tile0),
        out_shape=jax.ShapeDtypeStruct((lines // tile_rows, fields, tile_rows, cells), BF16),
        in_specs=[VMEM] * 5,
        out_specs=VMEM,
        compiler_params=params(),
        cost_estimate=cost(sweep_flops, 4 * array_bytes),
        name="last",
    )(consts, blocks, interior, ends, inv_y)
    back = lax.all_to_all(planes, "pen", split_axis=0, concat_axis=0, tiled=True, axis_index_groups=within)
    return from_planes(back)[None]


def solution(mesh):
    return jax.shard_map(
        local,
        mesh=mesh,
        in_specs=(
            P("blk", None, None, "pen", None),
            P("blk", None, None, None),
            P("blk", None, None, None),
            P("blk", None),
            P("blk", None),
            P("blk", None),
            P("blk", None),
            P("blk", None),
        ),
        out_specs=P("blk", None, None, "pen", None),
        check_vma=False,
    )
```

```python
import functools

import jax
import jax.numpy as jnp
from jax import lax
from jax.experimental import pallas as pl
from jax.experimental.pallas import tpu as pltpu
from jax.sharding import PartitionSpec as P

STEPS = 2
SLOT_ROWS = 4
F32 = jnp.float32
BF16 = jnp.bfloat16
VMEM = pl.BlockSpec(memory_space=pltpu.VMEM)
HBM = pl.BlockSpec(memory_space=pltpu.HBM)
SMEM = pl.BlockSpec(memory_space=pltpu.SMEM)
NT = (((1,), (1,)), ((), ()))
TN = (((0,), (0,)), ((), ()))


def turned_group(size, first):
    return [[(first + member) % size for member in range(size)]]


def params():
    return pltpu.CompilerParams(vmem_limit_bytes=16 * 1024 * 1024)


def rows_of(shape):
    return lax.broadcasted_iota(jnp.int32, shape, 0)


def transfer(pairs, sems):
    copies = [
        pltpu.make_async_copy(source, target, sems.at[number])
        for number, (source, target) in enumerate(pairs)
    ]
    for copy in copies:
        copy.start()
    for copy in copies:
        copy.wait()


def pieces_of(by_field, by_plane, parts):
    chunk = by_plane.shape[0] // parts
    return [
        (by_field.at[field, pl.ds(part * chunk, chunk)], by_plane.at[pl.ds(part * chunk, chunk), field])
        for part in range(parts)
        for field in range(2)
    ]


def from_planes_kernel(source, target, sems):
    transfer([(held, sent) for sent, held in pieces_of(target, source, 1)], sems)


def from_planes(moved):
    planes, fields, lines, cells = moved.shape
    return pl.pallas_call(
        from_planes_kernel,
        out_shape=jax.ShapeDtypeStruct((fields, planes, lines, cells), BF16),
        in_specs=[VMEM],
        out_specs=HBM,
        scratch_shapes=[pltpu.SemaphoreType.DMA((2,))],
        compiler_params=params(),
        name="from_planes",
    )(moved)


def in_order(tiles, first):
    count = tiles.shape[0]
    ordered = jnp.concatenate([tiles[count - first:], tiles[:count - first]], axis=0)
    return ordered.reshape(-1, tiles.shape[-1])


def shift_bits(lines, tile_rows):
    return (lines // tile_rows).bit_length() - 1


def stage_kernel(state, inv_x, planes, ends, probe, sides, tops, sems):
    cells = inv_x.shape[-1]
    pairs = pieces_of(state, planes, 1)
    for field in range(2):
        for end in range(2):
            pairs.append((inv_x.at[field, :, pl.ds(end * (cells - 128), 128)], sides.at[field, end]))
            pairs.append((inv_x.at[field, pl.ds(end * (cells - 16), 16)], tops.at[field, end]))
    copies = [
        pltpu.make_async_copy(source, target, sems.at[number])
        for number, (source, target) in enumerate(pairs)
    ]
    for copy in copies:
        copy.start()
    for copy in copies[2:]:
        copy.wait()

    lane = lax.broadcasted_iota(jnp.int32, (16, 256), 1)
    row = rows_of((16, 256))
    pick = ((row == 0) & (lane == 0)) | ((row == 1) & (lane == 255))
    pick = jnp.where(pick, 1.0, 0.0).astype(BF16)
    row = rows_of((16, cells))
    lane = lax.broadcasted_iota(jnp.int32, (16, cells), 1)
    hot = ((row == 2) & (lane == 0)) | ((row == 3) & (lane == cells - 1))
    hot = jnp.where(hot, 1.0, 0.0)
    for field in range(2):
        both = jnp.concatenate([sides[field, 0], sides[field, 1]], axis=1)
        ends[field] = lax.dot_general(pick, both, NT, preferred_element_type=F32).astype(BF16)
        first = tops[field, 0].astype(F32)[0:1]
        last = tops[field, 1].astype(F32)[15:16]
        probe[field] = jnp.where(row == 0, first, jnp.where(row == 1, last, hot)).astype(BF16)
    for copy in copies[:2]:
        copy.wait()


def layers_kernel(tile0, planes, probe, sent, corners):
    seen = []
    for field in range(2):
        plane = in_order(planes[:, field], tile0)
        seen.append(lax.dot_general(probe[field], plane, NT, preferred_element_type=F32)[0:8])
        corners[field] = seen[field]
    rows = [seen[field][2 + end:3 + end] for end in range(2) for field in range(2)]
    total = jnp.concatenate(rows, axis=0).astype(BF16)
    for slot in range(sent.shape[0]):
        sent[slot] = total


def spread(number, lines):
    return jnp.concatenate([jnp.broadcast_to(number, (1, 128))] * (lines // 128), axis=1)


def by_side(pair, lines):
    upper = rows_of((8, 128)) < 2
    low = jnp.broadcast_to(pair[0:1, 0:1], (8, 128))
    high = jnp.broadcast_to(pair[0:1, 1:2], (8, 128))
    return jnp.concatenate([jnp.where(upper, low, high)] * (lines // 128), axis=1)


def mirrored(layer):
    cells = layer.shape[-1]
    back = 127 - lax.broadcasted_iota(jnp.int32, (layer.shape[0], 128), 1)
    pieces = [
        jnp.take_along_axis(layer[:, at:at + 128], back, axis=1)
        for at in range(cells - 128, -1, -128)
    ]
    return jnp.concatenate(pieces, axis=1)


def ghost_rows(tables, blocks, origin, tile_rows):
    count, _, lines = blocks.shape
    partner, face_side, orient, offset = (by_side(table, lines) for table in tables)
    place = partner - origin
    place = jnp.where(place < 0, place + count, place)
    layers = []
    for which in range(2):
        wanted = place[2 * which:2 * which + 1]
        layer = blocks[0].astype(F32)
        for slot in range(1, count):
            layer = jnp.where(wanted == slot, blocks[slot].astype(F32), layer)
        layers.append(layer)
    near = jnp.concatenate([layers[0][0:2], layers[1][0:2]] * 2, axis=0)
    far = jnp.concatenate([layers[0][2:4], layers[1][2:4]] * 2, axis=0)
    rows = jnp.where(face_side == 1, far, near)
    for bit in range(shift_bits(lines, tile_rows)):
        moved = pltpu.roll(rows, lines - (tile_rows << bit), 1)
        rows = jnp.where((offset >> bit) & 1 == 1, moved, rows)
    return jnp.where(orient == 1, mirrored(rows), rows)


def packed_ghosts(found, field):
    row = rows_of((16, found.shape[-1]))
    low = found[field:field + 1]
    high = found[2 + field:3 + field]
    return jnp.where(row == 0, low, jnp.where(row == 1, high, 0.0)).astype(BF16)


def mix(rates, proton, carbon):
    lines = proton.shape[-1]
    first, second, cross = (spread(rates[0:1, at:at + 1], lines) for at in range(3))
    new_proton = proton - (first * proton + cross * carbon)
    new_carbon = carbon - (second * carbon + cross * proton)
    return new_proton, new_carbon


def next_layers_kernel(
    tile_rows, origin, rates, partner, face_side, orient, offset, blocks, corners, ends, inv_y, sent, ghosts):
    cells = ends.shape[-1]
    found = ghost_rows((partner, face_side, orient, offset), blocks, origin, tile_rows)
    row = rows_of((16, cells))
    swept = []
    for field in range(2):
        edge = ends[field].astype(F32)
        ghosts[field] = packed_ghosts(found, field)
        layers = []
        for end in range(2):
            lane = end * (cells - 1)
            value = corners[field][end:end + 1]
            for which in range(2):
                at = which * 2 + field
                value = value + edge[which:which + 1, lane:lane + 1] * found[at:at + 1]
            layers.append(value)
        two = jnp.where(row == 0, layers[0], jnp.where(row == 1, layers[1], 0.0)).astype(BF16)
        swept.append(lax.dot_general(two, inv_y[field], NT, preferred_element_type=F32)[0:8])
    new_proton, new_carbon = mix(rates, swept[0], swept[1])
    total = jnp.concatenate(
        [new_proton[0:1], new_carbon[0:1], new_proton[1:2], new_carbon[1:2]], axis=0
    ).astype(BF16)
    for slot in range(sent.shape[0]):
        sent[slot] = total


def second_sweep(rates, interior, ghosts, ends, inv_y, emit):
    lines = inv_y.shape[-2]
    swept = []
    for field in range(2):
        outer = lax.dot_general(ghosts[field], ends[field], TN, preferred_element_type=F32)
        swept.append((interior(field) + outer).astype(BF16))
    chunk = lines // 2
    for start in range(0, lines, chunk):
        moved = [
            jnp.dot(inv_y[field, start:start + chunk], swept[field], preferred_element_type=F32)
            for field in range(2)
        ]
        new = mix(rates, moved[0], moved[1])
        for field in range(2):
            emit(field, start, chunk, new[field].astype(BF16))


def middle_kernel(tile_rows, tile0, rates, planes, ghosts, ends, inv_y, inv_x, following):
    def interior(field):
        plane = in_order(planes[:, field], tile0)
        return lax.dot_general(plane, inv_x[field], NT, preferred_element_type=F32)

    def emit(field, start, chunk, values):
        rows = lax.dot_general(values, inv_x[field], NT, preferred_element_type=F32)
        rows = rows.astype(BF16).reshape(-1, tile_rows, rows.shape[-1])
        first = start // tile_rows
        following[first:first + rows.shape[0], field] = rows

    second_sweep(rates, interior, ghosts, ends, inv_y, emit)


def last_kernel(
    tile_rows, tile0, origin, rates, partner, face_side, orient, offset, blocks, interior, ends,
    inv_y, planes,
):
    found = ghost_rows((partner, face_side, orient, offset), blocks, origin, tile_rows)
    ghosts = [packed_ghosts(found, field) for field in range(2)]

    def whole(field):
        return interior[:, field].reshape(-1, interior.shape[-1]).astype(F32)

    def emit(field, start, chunk, values):
        count = planes.shape[0]
        for row in range(0, chunk, tile_rows):
            place = ((start + row) // tile_rows + count - tile0) % count
            planes[place, field] = values[row:row + tile_rows]

    second_sweep(rates, whole, ghosts, ends, inv_y, emit)


def cost(flops, nbytes):
    return pl.CostEstimate(flops=flops, bytes_accessed=nbytes, transcendentals=0)


def local(state, inverse_x, inverse_y, rates, partner, face_side, orient, offset):
    magnet = state[0]
    inv_x = inverse_x[0]
    inv_y = inverse_y[0]
    fields, depth, tile_rows, cells = magnet.shape
    lines = inv_y.shape[-1]
    count = lax.axis_size("blk")
    width = lax.axis_size("pen")
    tile0 = (width * 21) // 32
    origin = (count * 5) // 8
    across = turned_group(count, origin)
    within = turned_group(width, tile0)
    numbers = (rates, partner, face_side, orient, offset)
    slots = jax.ShapeDtypeStruct((count, SLOT_ROWS, lines), BF16)
    packed = jax.ShapeDtypeStruct((fields, 16, lines), BF16)
    sweep_flops = 2 * fields * lines * cells * cells
    array_bytes = 2 * fields * lines * cells

    staged, ends, probe = pl.pallas_call(
        stage_kernel,
        out_shape=(
            jax.ShapeDtypeStruct((depth, fields, tile_rows, cells), BF16),
            packed,
            packed,
        ),
        in_specs=[HBM] * 2,
        out_specs=(VMEM,) * 3,
        scratch_shapes=[
            pltpu.VMEM((fields, 2, cells, 128), BF16),
            pltpu.VMEM((fields, 2, 16, cells), BF16),
            pltpu.SemaphoreType.DMA((10,)),
        ],
        compiler_params=pltpu.CompilerParams(vmem_limit_bytes=52 * 1024 * 1024),
        name="stage",
    )(magnet, inv_x)
    moved = lax.all_to_all(staged, "pen", split_axis=0, concat_axis=0, tiled=True, axis_index_groups=within)
    sent, corners = pl.pallas_call(
        functools.partial(layers_kernel, tile0),
        out_shape=(slots, jax.ShapeDtypeStruct((fields, 8, lines), F32)),
        in_specs=[VMEM, VMEM],
        out_specs=(VMEM, VMEM),
        compiler_params=params(),
        cost_estimate=cost(sweep_flops // 16, array_bytes),
        name="layers",
    )(moved, probe)
    blocks = lax.all_to_all(sent, "blk", split_axis=0, concat_axis=0, tiled=True, axis_index_groups=across)
    sent, ghosts = pl.pallas_call(
        functools.partial(next_layers_kernel, tile_rows, origin),
        out_shape=(slots, packed),
        in_specs=[VMEM] * 9,
        out_specs=(VMEM, VMEM),
        compiler_params=params(),
        cost_estimate=cost(sweep_flops // 16, array_bytes),
        name="next_layers",
    )(*numbers, blocks, corners, ends, inv_y)
    blocks = lax.all_to_all(sent, "blk", split_axis=0, concat_axis=0, tiled=True, axis_index_groups=across)
    interior = pl.pallas_call(
        functools.partial(middle_kernel, tile_rows, tile0),
        out_shape=jax.ShapeDtypeStruct(moved.shape, BF16),
        input_output_aliases={1: 0},
        in_specs=[VMEM] * 6,
        out_specs=VMEM,
        compiler_params=params(),
        cost_estimate=cost(3 * sweep_flops, 4 * array_bytes),
        name="middle",
    )(rates, moved, ghosts, ends, inv_y, inv_x)
    planes = pl.pallas_call(
        functools.partial(last_kernel, tile_rows, tile0, origin),
        out_shape=jax.ShapeDtypeStruct((lines // tile_rows, fields, tile_rows, cells), BF16),
        in_specs=[VMEM] * 9,
        out_specs=VMEM,
        compiler_params=params(),
        cost_estimate=cost(sweep_flops, 4 * array_bytes),
        name="last",
    )(*numbers, blocks, interior, ends, inv_y)
    back = lax.all_to_all(planes, "pen", split_axis=0, concat_axis=0, tiled=True, axis_index_groups=within)
    return from_planes(back)[None]


def solution(mesh):
    return jax.shard_map(
        local,
        mesh=mesh,
        in_specs=(
            P("blk", None, None, "pen", None),
            P("blk", None, None, None),
            P("blk", None, None, None),
            P("blk", None),
            P("blk", None),
            P("blk", None),
            P("blk", None),
            P("blk", None),
        ),
        out_specs=P("blk", None, None, "pen", None),
        check_vma=False,
    )
```

```python
import functools

import jax
import jax.numpy as jnp
from jax import lax
from jax.experimental import pallas as pl
from jax.experimental.pallas import tpu as pltpu
from jax.sharding import PartitionSpec as P

STEPS = 2
SLOT_ROWS = 4
F32 = jnp.float32
BF16 = jnp.bfloat16
VMEM = pl.BlockSpec(memory_space=pltpu.VMEM)
HBM = pl.BlockSpec(memory_space=pltpu.HBM)
SMEM = pl.BlockSpec(memory_space=pltpu.SMEM)
NT = (((1,), (1,)), ((), ()))
TN = (((0,), (0,)), ((), ()))


def turned_group(size, first):
    return [[(first + member) % size for member in range(size)]]


def params():
    return pltpu.CompilerParams(vmem_limit_bytes=16 * 1024 * 1024)


def rows_of(shape):
    return lax.broadcasted_iota(jnp.int32, shape, 0)


def transfer(pairs, sems):
    copies = [
        pltpu.make_async_copy(source, target, sems.at[number])
        for number, (source, target) in enumerate(pairs)
    ]
    for copy in copies:
        copy.start()
    for copy in copies:
        copy.wait()


def pieces_of(by_field, by_plane, parts):
    chunk = by_plane.shape[0] // parts
    return [
        (by_field.at[field, pl.ds(part * chunk, chunk)], by_plane.at[pl.ds(part * chunk, chunk), field])
        for part in range(parts)
        for field in range(2)
    ]


def from_planes_kernel(source, target, sems):
    transfer([(held, sent) for sent, held in pieces_of(target, source, 1)], sems)


def from_planes(moved):
    planes, fields, lines, cells = moved.shape
    return pl.pallas_call(
        from_planes_kernel,
        out_shape=jax.ShapeDtypeStruct((fields, planes, lines, cells), BF16),
        in_specs=[VMEM],
        out_specs=HBM,
        scratch_shapes=[pltpu.SemaphoreType.DMA((2,))],
        compiler_params=params(),
        name="from_planes",
    )(moved)


def in_order(tiles, first):
    count = tiles.shape[0]
    ordered = jnp.concatenate([tiles[count - first:], tiles[:count - first]], axis=0)
    return ordered.reshape(-1, tiles.shape[-1])


def shift_bits(lines, tile_rows):
    return (lines // tile_rows).bit_length() - 1


def stage_kernel(state, inv_x, planes, probe, tops, sems):
    cells = inv_x.shape[-1]
    pairs = pieces_of(state, planes, 1)
    for field in range(2):
        for end in range(2):
            pairs.append((inv_x.at[field, pl.ds(end * (cells - 16), 16)], tops.at[field, end]))
    copies = [
        pltpu.make_async_copy(source, target, sems.at[number])
        for number, (source, target) in enumerate(pairs)
    ]
    for copy in copies:
        copy.start()
    for copy in copies[2:]:
        copy.wait()

    row = rows_of((16, cells))
    lane = lax.broadcasted_iota(jnp.int32, (16, cells), 1)
    hot = ((row == 2) & (lane == 0)) | ((row == 3) & (lane == cells - 1))
    hot = jnp.where(hot, 1.0, 0.0)
    for field in range(2):
        first = tops[field, 0].astype(F32)[0:1]
        last = tops[field, 1].astype(F32)[15:16]
        probe[field] = jnp.where(row == 0, first, jnp.where(row == 1, last, hot)).astype(BF16)
    for copy in copies[:2]:
        copy.wait()


def layers_kernel(tile0, planes, probe, sent, corners):
    seen = []
    for field in range(2):
        plane = in_order(planes[:, field], tile0)
        seen.append(lax.dot_general(probe[field], plane, NT, preferred_element_type=F32)[0:8])
        corners[field] = seen[field]
    rows = [seen[field][2 + end:3 + end] for end in range(2) for field in range(2)]
    total = jnp.concatenate(rows, axis=0).astype(BF16)
    for slot in range(sent.shape[0]):
        sent[slot] = total


def spread(number, lines):
    return jnp.concatenate([jnp.broadcast_to(number, (1, 128))] * (lines // 128), axis=1)


def by_side(pair, lines):
    upper = rows_of((8, 128)) < 2
    low = jnp.broadcast_to(pair[0:1, 0:1], (8, 128))
    high = jnp.broadcast_to(pair[0:1, 1:2], (8, 128))
    return jnp.concatenate([jnp.where(upper, low, high)] * (lines // 128), axis=1)


def mirrored(layer):
    cells = layer.shape[-1]
    back = 127 - lax.broadcasted_iota(jnp.int32, (layer.shape[0], 128), 1)
    pieces = [
        jnp.take_along_axis(layer[:, at:at + 128], back, axis=1)
        for at in range(cells - 128, -1, -128)
    ]
    return jnp.concatenate(pieces, axis=1)


def ghost_rows(tables, blocks, origin, tile_rows):
    count, _, lines = blocks.shape
    partner, face_side, orient, offset = (by_side(table, lines) for table in tables)
    place = partner - origin
    place = jnp.where(place < 0, place + count, place)
    layers = []
    for which in range(2):
        wanted = place[2 * which:2 * which + 1]
        layer = blocks[0].astype(F32)
        for slot in range(1, count):
            layer = jnp.where(wanted == slot, blocks[slot].astype(F32), layer)
        layers.append(layer)
    near = jnp.concatenate([layers[0][0:2], layers[1][0:2]] * 2, axis=0)
    far = jnp.concatenate([layers[0][2:4], layers[1][2:4]] * 2, axis=0)
    rows = jnp.where(face_side == 1, far, near)
    for bit in range(shift_bits(lines, tile_rows)):
        moved = pltpu.roll(rows, lines - (tile_rows << bit), 1)
        rows = jnp.where((offset >> bit) & 1 == 1, moved, rows)
    return jnp.where(orient == 1, mirrored(rows), rows)


def packed_ghosts(found, field):
    row = rows_of((16, found.shape[-1]))
    low = found[field:field + 1]
    high = found[2 + field:3 + field]
    return jnp.where(row == 0, low, jnp.where(row == 1, high, 0.0)).astype(BF16)


def mix(rates, proton, carbon):
    lines = proton.shape[-1]
    first, second, cross = (spread(rates[0:1, at:at + 1], lines) for at in range(3))
    new_proton = proton - (first * proton + cross * carbon)
    new_carbon = carbon - (second * carbon + cross * proton)
    return new_proton, new_carbon


def next_layers_kernel(
    tile_rows, origin, rates, partner, face_side, orient, offset, blocks, corners, probe, inv_y, sent, ghosts):
    cells = probe.shape[-1]
    found = ghost_rows((partner, face_side, orient, offset), blocks, origin, tile_rows)
    row = rows_of((16, cells))
    swept = []
    for field in range(2):
        edge = probe[field].astype(F32)
        ghosts[field] = packed_ghosts(found, field)
        layers = []
        for end in range(2):
            value = corners[field][end:end + 1]
            for which in range(2):
                at = which * 2 + field
                lane = which * (cells - 1)
                value = value + edge[end:end + 1, lane:lane + 1] * found[at:at + 1]
            layers.append(value)
        two = jnp.where(row == 0, layers[0], jnp.where(row == 1, layers[1], 0.0)).astype(BF16)
        swept.append(lax.dot_general(two, inv_y[field], NT, preferred_element_type=F32)[0:8])
    new_proton, new_carbon = mix(rates, swept[0], swept[1])
    total = jnp.concatenate(
        [new_proton[0:1], new_carbon[0:1], new_proton[1:2], new_carbon[1:2]], axis=0
    ).astype(BF16)
    for slot in range(sent.shape[0]):
        sent[slot] = total


def second_sweep(rates, interior, ghosts, ends, inv_y, emit):
    lines = inv_y.shape[-2]
    swept = []
    for field in range(2):
        outer = lax.dot_general(ghosts[field], ends[field], TN, preferred_element_type=F32)
        swept.append((interior(field) + outer).astype(BF16))
    chunk = lines // 2
    for start in range(0, lines, chunk):
        moved = [
            jnp.dot(inv_y[field, start:start + chunk], swept[field], preferred_element_type=F32)
            for field in range(2)
        ]
        new = mix(rates, moved[0], moved[1])
        for field in range(2):
            emit(field, start, chunk, new[field].astype(BF16))


def middle_kernel(tile_rows, tile0, rates, planes, ghosts, inv_y, inv_x, following, ends):
    cells = inv_x.shape[-1]
    row = rows_of((16, cells))
    lane = lax.broadcasted_iota(jnp.int32, (16, cells), 1)
    pick = ((row == 0) & (lane == 0)) | ((row == 1) & (lane == cells - 1))
    pick = jnp.where(pick, 1.0, 0.0).astype(BF16)
    columns = [
        lax.dot_general(pick, inv_x[field], NT, preferred_element_type=F32).astype(BF16)
        for field in range(2)
    ]
    for field in range(2):
        ends[field] = columns[field]

    def interior(field):
        plane = in_order(planes[:, field], tile0)
        return lax.dot_general(plane, inv_x[field], NT, preferred_element_type=F32)

    def emit(field, start, chunk, values):
        rows = lax.dot_general(values, inv_x[field], NT, preferred_element_type=F32)
        rows = rows.astype(BF16).reshape(-1, tile_rows, rows.shape[-1])
        first = start // tile_rows
        following[first:first + rows.shape[0], field] = rows

    second_sweep(rates, interior, ghosts, columns, inv_y, emit)


def last_kernel(
    tile_rows, tile0, origin, rates, partner, face_side, orient, offset, blocks, interior, ends,
    inv_y, planes,
):
    found = ghost_rows((partner, face_side, orient, offset), blocks, origin, tile_rows)
    ghosts = [packed_ghosts(found, field) for field in range(2)]

    def whole(field):
        return interior[:, field].reshape(-1, interior.shape[-1]).astype(F32)

    def emit(field, start, chunk, values):
        count = planes.shape[0]
        for row in range(0, chunk, tile_rows):
            place = ((start + row) // tile_rows + count - tile0) % count
            planes[place, field] = values[row:row + tile_rows]

    second_sweep(rates, whole, ghosts, ends, inv_y, emit)


def cost(flops, nbytes):
    return pl.CostEstimate(flops=flops, bytes_accessed=nbytes, transcendentals=0)


def local(state, inverse_x, inverse_y, rates, partner, face_side, orient, offset):
    magnet = state[0]
    inv_x = inverse_x[0]
    inv_y = inverse_y[0]
    fields, depth, tile_rows, cells = magnet.shape
    lines = inv_y.shape[-1]
    count = lax.axis_size("blk")
    width = lax.axis_size("pen")
    tile0 = (width * 21) // 32
    origin = (count * 5) // 8
    across = turned_group(count, origin)
    within = turned_group(width, tile0)
    numbers = (rates, partner, face_side, orient, offset)
    slots = jax.ShapeDtypeStruct((count, SLOT_ROWS, lines), BF16)
    packed = jax.ShapeDtypeStruct((fields, 16, lines), BF16)
    sweep_flops = 2 * fields * lines * cells * cells
    array_bytes = 2 * fields * lines * cells

    staged, probe = pl.pallas_call(
        stage_kernel,
        out_shape=(
            jax.ShapeDtypeStruct((depth, fields, tile_rows, cells), BF16),
            packed,
        ),
        in_specs=[HBM] * 2,
        out_specs=(VMEM,) * 2,
        scratch_shapes=[
            pltpu.VMEM((fields, 2, 16, cells), BF16),
            pltpu.SemaphoreType.DMA((6,)),
        ],
        compiler_params=pltpu.CompilerParams(vmem_limit_bytes=52 * 1024 * 1024),
        name="stage",
    )(magnet, inv_x)
    moved = lax.all_to_all(staged, "pen", split_axis=0, concat_axis=0, tiled=True, axis_index_groups=within)
    sent, corners = pl.pallas_call(
        functools.partial(layers_kernel, tile0),
        out_shape=(slots, jax.ShapeDtypeStruct((fields, 8, lines), F32)),
        in_specs=[VMEM, VMEM],
        out_specs=(VMEM, VMEM),
        compiler_params=params(),
        cost_estimate=cost(sweep_flops // 16, array_bytes),
        name="layers",
    )(moved, probe)
    blocks = lax.all_to_all(sent, "blk", split_axis=0, concat_axis=0, tiled=True, axis_index_groups=across)
    sent, ghosts = pl.pallas_call(
        functools.partial(next_layers_kernel, tile_rows, origin),
        out_shape=(slots, packed),
        in_specs=[VMEM] * 9,
        out_specs=(VMEM, VMEM),
        compiler_params=params(),
        cost_estimate=cost(sweep_flops // 16, array_bytes),
        name="next_layers",
    )(*numbers, blocks, corners, probe, inv_y)
    blocks = lax.all_to_all(sent, "blk", split_axis=0, concat_axis=0, tiled=True, axis_index_groups=across)
    interior, ends = pl.pallas_call(
        functools.partial(middle_kernel, tile_rows, tile0),
        out_shape=(jax.ShapeDtypeStruct(moved.shape, BF16), packed),
        input_output_aliases={1: 0},
        in_specs=[VMEM] * 5,
        out_specs=(VMEM, VMEM),
        compiler_params=params(),
        cost_estimate=cost(3 * sweep_flops, 4 * array_bytes),
        name="middle",
    )(rates, moved, ghosts, inv_y, inv_x)
    planes = pl.pallas_call(
        functools.partial(last_kernel, tile_rows, tile0, origin),
        out_shape=jax.ShapeDtypeStruct((lines // tile_rows, fields, tile_rows, cells), BF16),
        in_specs=[VMEM] * 9,
        out_specs=VMEM,
        compiler_params=params(),
        cost_estimate=cost(sweep_flops, 4 * array_bytes),
        name="last",
    )(*numbers, blocks, interior, ends, inv_y)
    back = lax.all_to_all(planes, "pen", split_axis=0, concat_axis=0, tiled=True, axis_index_groups=within)
    return from_planes(back)[None]


def solution(mesh):
    return jax.shard_map(
        local,
        mesh=mesh,
        in_specs=(
            P("blk", None, None, "pen", None),
            P("blk", None, None, None),
            P("blk", None, None, None),
            P("blk", None),
            P("blk", None),
            P("blk", None),
            P("blk", None),
            P("blk", None),
        ),
        out_specs=P("blk", None, None, "pen", None),
        check_vma=False,
    )
```

```python
import functools

import jax
import jax.numpy as jnp
from jax import lax
from jax.experimental import pallas as pl
from jax.experimental.pallas import tpu as pltpu
from jax.sharding import PartitionSpec as P

STEPS = 2
SLOT_ROWS = 4
F32 = jnp.float32
BF16 = jnp.bfloat16
VMEM = pl.BlockSpec(memory_space=pltpu.VMEM)
HBM = pl.BlockSpec(memory_space=pltpu.HBM)
SMEM = pl.BlockSpec(memory_space=pltpu.SMEM)
NT = (((1,), (1,)), ((), ()))
TN = (((0,), (0,)), ((), ()))


def turned_group(size, first):
    return [[(first + member) % size for member in range(size)]]


def params():
    return pltpu.CompilerParams(vmem_limit_bytes=16 * 1024 * 1024)


def rows_of(shape):
    return lax.broadcasted_iota(jnp.int32, shape, 0)


def transfer(pairs, sems):
    copies = [
        pltpu.make_async_copy(source, target, sems.at[number])
        for number, (source, target) in enumerate(pairs)
    ]
    for copy in copies:
        copy.start()
    for copy in copies:
        copy.wait()


def pieces_of(by_field, by_plane, parts):
    chunk = by_plane.shape[0] // parts
    return [
        (by_field.at[field, pl.ds(part * chunk, chunk)], by_plane.at[pl.ds(part * chunk, chunk), field])
        for part in range(parts)
        for field in range(2)
    ]


def from_planes_kernel(source, target, sems):
    transfer([(held, sent) for sent, held in pieces_of(target, source, 1)], sems)


def from_planes(moved):
    planes, fields, lines, cells = moved.shape
    return pl.pallas_call(
        from_planes_kernel,
        out_shape=jax.ShapeDtypeStruct((fields, planes, lines, cells), BF16),
        in_specs=[VMEM],
        out_specs=HBM,
        scratch_shapes=[pltpu.SemaphoreType.DMA((2,))],
        compiler_params=params(),
        name="from_planes",
    )(moved)


def in_order(tiles, first):
    count = tiles.shape[0]
    ordered = jnp.concatenate([tiles[count - first:], tiles[:count - first]], axis=0)
    return ordered.reshape(-1, tiles.shape[-1])


def shift_bits(lines, tile_rows):
    return (lines // tile_rows).bit_length() - 1


def stage_kernel(state, inv_x, planes, probe, tops, sems):
    cells = inv_x.shape[-1]
    pairs = pieces_of(state, planes, 1)
    for field in range(2):
        for end in range(2):
            pairs.append((inv_x.at[field, pl.ds(end * (cells - 16), 16)], tops.at[field, end]))
    copies = [
        pltpu.make_async_copy(source, target, sems.at[number])
        for number, (source, target) in enumerate(pairs)
    ]
    for copy in copies:
        copy.start()
    for copy in copies[2:]:
        copy.wait()

    row = rows_of((16, cells))
    lane = lax.broadcasted_iota(jnp.int32, (16, cells), 1)
    hot = ((row == 2) & (lane == 0)) | ((row == 3) & (lane == cells - 1))
    hot = jnp.where(hot, 1.0, 0.0)
    for field in range(2):
        first = tops[field, 0].astype(F32)[0:1]
        last = tops[field, 1].astype(F32)[15:16]
        probe[field] = jnp.where(row == 0, first, jnp.where(row == 1, last, hot)).astype(BF16)
    for copy in copies[:2]:
        copy.wait()


def layers_kernel(tile0, planes, probe, sent, corners):
    seen = []
    for field in range(2):
        plane = in_order(planes[:, field], tile0)
        seen.append(lax.dot_general(probe[field], plane, NT, preferred_element_type=F32)[0:8])
        corners[field] = seen[field]
    rows = [seen[field][2 + end:3 + end] for end in range(2) for field in range(2)]
    total = jnp.concatenate(rows, axis=0).astype(BF16)
    for slot in range(sent.shape[0]):
        sent[slot] = total


def spread(number, lines):
    return jnp.concatenate([jnp.broadcast_to(number, (1, 128))] * (lines // 128), axis=1)


def by_side(pair, lines):
    upper = rows_of((8, 128)) < 2
    low = jnp.broadcast_to(pair[0:1, 0:1], (8, 128))
    high = jnp.broadcast_to(pair[0:1, 1:2], (8, 128))
    return jnp.concatenate([jnp.where(upper, low, high)] * (lines // 128), axis=1)


def mirrored(layer):
    cells = layer.shape[-1]
    back = 127 - lax.broadcasted_iota(jnp.int32, (layer.shape[0], 128), 1)
    pieces = [
        jnp.take_along_axis(layer[:, at:at + 128], back, axis=1)
        for at in range(cells - 128, -1, -128)
    ]
    return jnp.concatenate(pieces, axis=1)


def spread_tables(tables, count, lines, origin, tile_rows):
    partner, face_side, orient, offset = (by_side(table, 128) for table in tables)
    place = partner - origin
    place = jnp.where(place < 0, place + count, place)
    bits = (lines // tile_rows).bit_length() - 1
    return [place, face_side, orient, *((offset >> bit) & 1 for bit in range(bits))]


def ghost_rows(spreads, blocks, tile_rows):
    count, _, lines = blocks.shape
    place, face_side, orient, *bits = (
        jnp.concatenate([piece] * (lines // 128), axis=1) for piece in spreads
    )
    layers = []
    for which in range(2):
        wanted = place[2 * which:2 * which + 1]
        layer = blocks[0].astype(F32)
        for slot in range(1, count):
            layer = jnp.where(wanted == slot, blocks[slot].astype(F32), layer)
        layers.append(layer)
    near = jnp.concatenate([layers[0][0:2], layers[1][0:2]] * 2, axis=0)
    far = jnp.concatenate([layers[0][2:4], layers[1][2:4]] * 2, axis=0)
    rows = jnp.where(face_side == 1, far, near)
    for bit, mark in enumerate(bits):
        moved = pltpu.roll(rows, lines - (tile_rows << bit), 1)
        rows = jnp.where(mark == 1, moved, rows)
    return jnp.where(orient == 1, mirrored(rows), rows)


def packed_ghosts(found, field):
    row = rows_of((16, found.shape[-1]))
    low = found[field:field + 1]
    high = found[2 + field:3 + field]
    return jnp.where(row == 0, low, jnp.where(row == 1, high, 0.0)).astype(BF16)


def mix(rates, proton, carbon):
    lines = proton.shape[-1]
    first, second, cross = (spread(rates[0:1, at:at + 1], lines) for at in range(3))
    new_proton = proton - (first * proton + cross * carbon)
    new_carbon = carbon - (second * carbon + cross * proton)
    return new_proton, new_carbon


def next_layers_kernel(
    tile_rows, origin, rates, partner, face_side, orient, offset, blocks, corners, probe, inv_y, sent, ghosts):
    cells = probe.shape[-1]
    tables = (partner, face_side, orient, offset)
    spreads = spread_tables(tables, blocks.shape[0], cells, origin, tile_rows)
    found = ghost_rows(spreads, blocks, tile_rows)
    row = rows_of((16, cells))
    swept = []
    for field in range(2):
        edge = probe[field].astype(F32)
        ghosts[field] = packed_ghosts(found, field)
        layers = []
        for end in range(2):
            value = corners[field][end:end + 1]
            for which in range(2):
                at = which * 2 + field
                lane = which * (cells - 1)
                value = value + edge[end:end + 1, lane:lane + 1] * found[at:at + 1]
            layers.append(value)
        two = jnp.where(row == 0, layers[0], jnp.where(row == 1, layers[1], 0.0)).astype(BF16)
        swept.append(lax.dot_general(two, inv_y[field], NT, preferred_element_type=F32)[0:8])
    new_proton, new_carbon = mix(rates, swept[0], swept[1])
    total = jnp.concatenate(
        [new_proton[0:1], new_carbon[0:1], new_proton[1:2], new_carbon[1:2]], axis=0
    ).astype(BF16)
    for slot in range(sent.shape[0]):
        sent[slot] = total


def second_sweep(rates, interior, ghosts, ends, inv_y, emit):
    lines = inv_y.shape[-2]
    swept = []
    for field in range(2):
        outer = lax.dot_general(ghosts[field], ends[field], TN, preferred_element_type=F32)
        swept.append((interior(field) + outer).astype(BF16))
    chunk = lines // 2
    for start in range(0, lines, chunk):
        moved = [
            jnp.dot(inv_y[field, start:start + chunk], swept[field], preferred_element_type=F32)
            for field in range(2)
        ]
        new = mix(rates, moved[0], moved[1])
        for field in range(2):
            emit(field, start, chunk, new[field].astype(BF16))


def middle_kernel(
    tile_rows, tile0, origin, count, rates, partner, face_side, orient, offset, planes, ghosts,
    inv_y, inv_x, following, ends, marks,
):
    cells = inv_x.shape[-1]
    row = rows_of((16, cells))
    lane = lax.broadcasted_iota(jnp.int32, (16, cells), 1)
    pick = ((row == 0) & (lane == 0)) | ((row == 1) & (lane == cells - 1))
    pick = jnp.where(pick, 1.0, 0.0).astype(BF16)
    columns = [
        lax.dot_general(pick, inv_x[field], NT, preferred_element_type=F32).astype(BF16)
        for field in range(2)
    ]
    for field in range(2):
        ends[field] = columns[field]
    tables = (partner, face_side, orient, offset)
    for at, piece in enumerate(spread_tables(tables, count, cells, origin, tile_rows)):
        marks[at] = piece

    def interior(field):
        plane = in_order(planes[:, field], tile0)
        return lax.dot_general(plane, inv_x[field], NT, preferred_element_type=F32)

    def emit(field, start, chunk, values):
        rows = lax.dot_general(values, inv_x[field], NT, preferred_element_type=F32)
        rows = rows.astype(BF16).reshape(-1, tile_rows, rows.shape[-1])
        first = start // tile_rows
        following[first:first + rows.shape[0], field] = rows

    second_sweep(rates, interior, ghosts, columns, inv_y, emit)


def last_kernel(tile_rows, tile0, rates, marks, blocks, interior, ends, inv_y, planes):
    found = ghost_rows([marks[at] for at in range(marks.shape[0])], blocks, tile_rows)
    ghosts = [packed_ghosts(found, field) for field in range(2)]

    def whole(field):
        return interior[:, field].reshape(-1, interior.shape[-1]).astype(F32)

    def emit(field, start, chunk, values):
        count = planes.shape[0]
        for row in range(0, chunk, tile_rows):
            place = ((start + row) // tile_rows + count - tile0) % count
            planes[place, field] = values[row:row + tile_rows]

    second_sweep(rates, whole, ghosts, ends, inv_y, emit)


def cost(flops, nbytes):
    return pl.CostEstimate(flops=flops, bytes_accessed=nbytes, transcendentals=0)


def local(state, inverse_x, inverse_y, rates, partner, face_side, orient, offset):
    magnet = state[0]
    inv_x = inverse_x[0]
    inv_y = inverse_y[0]
    fields, depth, tile_rows, cells = magnet.shape
    lines = inv_y.shape[-1]
    count = lax.axis_size("blk")
    width = lax.axis_size("pen")
    tile0 = (width * 21) // 32
    origin = (count * 5) // 8
    across = turned_group(count, origin)
    within = turned_group(width, tile0)
    numbers = (rates, partner, face_side, orient, offset)
    slots = jax.ShapeDtypeStruct((count, SLOT_ROWS, lines), BF16)
    packed = jax.ShapeDtypeStruct((fields, 16, lines), BF16)
    sweep_flops = 2 * fields * lines * cells * cells
    array_bytes = 2 * fields * lines * cells

    staged, probe = pl.pallas_call(
        stage_kernel,
        out_shape=(
            jax.ShapeDtypeStruct((depth, fields, tile_rows, cells), BF16),
            packed,
        ),
        in_specs=[HBM] * 2,
        out_specs=(VMEM,) * 2,
        scratch_shapes=[
            pltpu.VMEM((fields, 2, 16, cells), BF16),
            pltpu.SemaphoreType.DMA((6,)),
        ],
        compiler_params=pltpu.CompilerParams(vmem_limit_bytes=52 * 1024 * 1024),
        name="stage",
    )(magnet, inv_x)
    moved = lax.all_to_all(staged, "pen", split_axis=0, concat_axis=0, tiled=True, axis_index_groups=within)
    sent, corners = pl.pallas_call(
        functools.partial(layers_kernel, tile0),
        out_shape=(slots, jax.ShapeDtypeStruct((fields, 8, lines), F32)),
        in_specs=[VMEM, VMEM],
        out_specs=(VMEM, VMEM),
        compiler_params=params(),
        cost_estimate=cost(sweep_flops // 16, array_bytes),
        name="layers",
    )(moved, probe)
    blocks = lax.all_to_all(sent, "blk", split_axis=0, concat_axis=0, tiled=True, axis_index_groups=across)
    sent, ghosts = pl.pallas_call(
        functools.partial(next_layers_kernel, tile_rows, origin),
        out_shape=(slots, packed),
        in_specs=[VMEM] * 9,
        out_specs=(VMEM, VMEM),
        compiler_params=params(),
        cost_estimate=cost(sweep_flops // 16, array_bytes),
        name="next_layers",
    )(*numbers, blocks, corners, probe, inv_y)
    blocks = lax.all_to_all(sent, "blk", split_axis=0, concat_axis=0, tiled=True, axis_index_groups=across)
    marks = 3 + (lines // tile_rows).bit_length() - 1
    interior, ends, marks = pl.pallas_call(
        functools.partial(middle_kernel, tile_rows, tile0, origin, count),
        out_shape=(
            jax.ShapeDtypeStruct(moved.shape, BF16),
            packed,
            jax.ShapeDtypeStruct((marks, 8, 128), jnp.int32),
        ),
        input_output_aliases={5: 0},
        in_specs=[VMEM] * 9,
        out_specs=(VMEM, VMEM, VMEM),
        compiler_params=params(),
        cost_estimate=cost(3 * sweep_flops, 4 * array_bytes),
        name="middle",
    )(*numbers, moved, ghosts, inv_y, inv_x)
    planes = pl.pallas_call(
        functools.partial(last_kernel, tile_rows, tile0),
        out_shape=jax.ShapeDtypeStruct((lines // tile_rows, fields, tile_rows, cells), BF16),
        in_specs=[VMEM] * 6,
        out_specs=VMEM,
        compiler_params=params(),
        cost_estimate=cost(sweep_flops, 4 * array_bytes),
        name="last",
    )(rates, marks, blocks, interior, ends, inv_y)
    back = lax.all_to_all(planes, "pen", split_axis=0, concat_axis=0, tiled=True, axis_index_groups=within)
    return from_planes(back)[None]


def solution(mesh):
    return jax.shard_map(
        local,
        mesh=mesh,
        in_specs=(
            P("blk", None, None, "pen", None),
            P("blk", None, None, None),
            P("blk", None, None, None),
            P("blk", None),
            P("blk", None),
            P("blk", None),
            P("blk", None),
            P("blk", None),
        ),
        out_specs=P("blk", None, None, "pen", None),
        check_vma=False,
    )
```

```python
import functools

import jax
import jax.numpy as jnp
from jax import lax
from jax.experimental import pallas as pl
from jax.experimental.pallas import tpu as pltpu
from jax.sharding import PartitionSpec as P

STEPS = 2
SLOT_ROWS = 4
F32 = jnp.float32
BF16 = jnp.bfloat16
VMEM = pl.BlockSpec(memory_space=pltpu.VMEM)
HBM = pl.BlockSpec(memory_space=pltpu.HBM)
SMEM = pl.BlockSpec(memory_space=pltpu.SMEM)
NT = (((1,), (1,)), ((), ()))
TN = (((0,), (0,)), ((), ()))


def turned_group(size, first):
    return [[(first + member) % size for member in range(size)]]


def params():
    return pltpu.CompilerParams(vmem_limit_bytes=16 * 1024 * 1024)


def rows_of(shape):
    return lax.broadcasted_iota(jnp.int32, shape, 0)


def transfer(pairs, sems):
    copies = [
        pltpu.make_async_copy(source, target, sems.at[number])
        for number, (source, target) in enumerate(pairs)
    ]
    for copy in copies:
        copy.start()
    for copy in copies:
        copy.wait()


def pieces_of(by_field, by_plane, parts):
    chunk = by_plane.shape[0] // parts
    return [
        (by_field.at[field, pl.ds(part * chunk, chunk)], by_plane.at[pl.ds(part * chunk, chunk), field])
        for part in range(parts)
        for field in range(2)
    ]


def from_planes_kernel(source, target, sems):
    transfer([(held, sent) for sent, held in pieces_of(target, source, 1)], sems)


def from_planes(moved):
    planes, fields, lines, cells = moved.shape
    return pl.pallas_call(
        from_planes_kernel,
        out_shape=jax.ShapeDtypeStruct((fields, planes, lines, cells), BF16),
        in_specs=[VMEM],
        out_specs=HBM,
        scratch_shapes=[pltpu.SemaphoreType.DMA((2,))],
        compiler_params=params(),
        name="from_planes",
    )(moved)


def in_order(tiles, first):
    count = tiles.shape[0]
    ordered = jnp.concatenate([tiles[count - first:], tiles[:count - first]], axis=0)
    return ordered.reshape(-1, tiles.shape[-1])


def shift_bits(lines, tile_rows):
    return (lines // tile_rows).bit_length() - 1


def stage_kernel(state, inv_x, planes, probe, tops, sems):
    cells = inv_x.shape[-1]
    pairs = pieces_of(state, planes, 1)
    for field in range(2):
        for end in range(2):
            pairs.append((inv_x.at[field, pl.ds(end * (cells - 16), 16)], tops.at[field, end]))
    copies = [
        pltpu.make_async_copy(source, target, sems.at[number])
        for number, (source, target) in enumerate(pairs)
    ]
    for copy in copies:
        copy.start()
    for copy in copies[2:]:
        copy.wait()

    row = rows_of((16, cells))
    lane = lax.broadcasted_iota(jnp.int32, (16, cells), 1)
    hot = ((row == 2) & (lane == 0)) | ((row == 3) & (lane == cells - 1))
    hot = jnp.where(hot, 1.0, 0.0)
    for field in range(2):
        first = tops[field, 0].astype(F32)[0:1]
        last = tops[field, 1].astype(F32)[15:16]
        probe[field] = jnp.where(row == 0, first, jnp.where(row == 1, last, hot)).astype(BF16)
    for copy in copies[:2]:
        copy.wait()


def layers_kernel(tile0, planes, probe, sent, corners):
    seen = []
    for field in range(2):
        plane = in_order(planes[:, field], tile0)
        seen.append(lax.dot_general(probe[field], plane, NT, preferred_element_type=F32)[0:8])
        corners[field] = seen[field]
    rows = [seen[field][2 + end:3 + end] for end in range(2) for field in range(2)]
    total = jnp.concatenate(rows, axis=0).astype(BF16)
    for slot in range(sent.shape[0]):
        sent[slot] = total


def spread(number, lines):
    return jnp.concatenate([jnp.broadcast_to(number, (1, 128))] * (lines // 128), axis=1)


def by_side(pair, lines):
    upper = rows_of((8, 128)) < 2
    low = jnp.broadcast_to(pair[0:1, 0:1], (8, 128))
    high = jnp.broadcast_to(pair[0:1, 1:2], (8, 128))
    return jnp.concatenate([jnp.where(upper, low, high)] * (lines // 128), axis=1)


def mirrored(layer):
    cells = layer.shape[-1]
    back = 127 - lax.broadcasted_iota(jnp.int32, (layer.shape[0], 128), 1)
    pieces = [
        jnp.take_along_axis(layer[:, at:at + 128], back, axis=1)
        for at in range(cells - 128, -1, -128)
    ]
    return jnp.concatenate(pieces, axis=1)


def spread_tables(tables, count, lines, origin, tile_rows):
    partner, face_side, orient, offset = (by_side(table, 128) for table in tables)
    place = partner - origin
    place = jnp.where(place < 0, place + count, place)
    bits = (lines // tile_rows).bit_length() - 1
    return [place, face_side, orient, *((offset >> bit) & 1 for bit in range(bits))]


def ghost_rows(spreads, blocks, tile_rows):
    count, _, lines = blocks.shape
    place, face_side, orient, *bits = (
        jnp.concatenate([piece] * (lines // 128), axis=1) for piece in spreads
    )
    layers = []
    for which in range(2):
        wanted = place[2 * which:2 * which + 1]
        layer = blocks[0].astype(F32)
        for slot in range(1, count):
            layer = jnp.where(wanted == slot, blocks[slot].astype(F32), layer)
        layers.append(layer)
    near = jnp.concatenate([layers[0][0:2], layers[1][0:2]] * 2, axis=0)
    far = jnp.concatenate([layers[0][2:4], layers[1][2:4]] * 2, axis=0)
    rows = jnp.where(face_side == 1, far, near)
    for bit, mark in enumerate(bits):
        moved = pltpu.roll(rows, lines - (tile_rows << bit), 1)
        rows = jnp.where(mark == 1, moved, rows)
    return jnp.where(orient == 1, mirrored(rows), rows)


def packed_ghosts(found, field):
    row = rows_of((16, found.shape[-1]))
    low = found[field:field + 1]
    high = found[2 + field:3 + field]
    return jnp.where(row == 0, low, jnp.where(row == 1, high, 0.0)).astype(BF16)


def mix(rates, proton, carbon):
    lines = proton.shape[-1]
    first, second, cross = (spread(rates[0:1, at:at + 1], lines) for at in range(3))
    new_proton = proton - (first * proton + cross * carbon)
    new_carbon = carbon - (second * carbon + cross * proton)
    return new_proton, new_carbon


def next_layers_kernel(
    tile_rows, origin, rates, partner, face_side, orient, offset, blocks, corners, probe, inv_y, sent, ghosts):
    cells = probe.shape[-1]
    tables = (partner, face_side, orient, offset)
    spreads = spread_tables(tables, blocks.shape[0], cells, origin, tile_rows)
    found = ghost_rows(spreads, blocks, tile_rows)
    row = rows_of((16, cells))
    swept = []
    for field in range(2):
        edge = probe[field].astype(F32)
        ghosts[field] = packed_ghosts(found, field)
        layers = []
        for end in range(2):
            value = corners[field][end:end + 1]
            for which in range(2):
                at = which * 2 + field
                lane = which * (cells - 1)
                value = value + edge[end:end + 1, lane:lane + 1] * found[at:at + 1]
            layers.append(value)
        two = jnp.where(row == 0, layers[0], jnp.where(row == 1, layers[1], 0.0)).astype(BF16)
        swept.append(lax.dot_general(two, inv_y[field], NT, preferred_element_type=F32)[0:8])
    new_proton, new_carbon = mix(rates, swept[0], swept[1])
    total = jnp.concatenate(
        [new_proton[0:1], new_carbon[0:1], new_proton[1:2], new_carbon[1:2]], axis=0
    ).astype(BF16)
    for slot in range(sent.shape[0]):
        sent[slot] = total


def second_sweep(rates, interior, ghosts, ends, inv_y, emit):
    lines = inv_y.shape[-2]
    swept = []
    for field in range(2):
        outer = lax.dot_general(ghosts[field], ends[field], TN, preferred_element_type=F32)
        swept.append((interior(field) + outer).astype(BF16))
    chunk = lines // 2
    for start in range(0, lines, chunk):
        moved = [
            jnp.dot(inv_y[field, start:start + chunk], swept[field], preferred_element_type=F32)
            for field in range(2)
        ]
        new = mix(rates, moved[0], moved[1])
        for field in range(2):
            emit(field, start, chunk, new[field].astype(BF16))


def middle_kernel(
    tile_rows, tile0, origin, count, rates, partner, face_side, orient, offset, planes, ghosts,
    inv_y, inv_x, following, ends, marks,
):
    cells = inv_x.shape[-1]
    row = rows_of((16, cells))
    lane = lax.broadcasted_iota(jnp.int32, (16, cells), 1)
    pick = ((row == 0) & (lane == 0)) | ((row == 1) & (lane == cells - 1))
    pick = jnp.where(pick, 1.0, 0.0).astype(BF16)
    columns = [
        lax.dot_general(pick, inv_x[field], NT, preferred_element_type=F32).astype(BF16)
        for field in range(2)
    ]
    for field in range(2):
        ends[field] = columns[field]
    tables = (partner, face_side, orient, offset)
    for at, piece in enumerate(spread_tables(tables, count, cells, origin, tile_rows)):
        marks[at] = piece

    def interior(field):
        plane = in_order(planes[:, field], tile0)
        return lax.dot_general(plane, inv_x[field], NT, preferred_element_type=F32)

    def emit(field, start, chunk, values):
        rows = lax.dot_general(values, inv_x[field], NT, preferred_element_type=F32)
        rows = rows.astype(BF16).reshape(-1, tile_rows, rows.shape[-1])
        first = start // tile_rows
        following[first:first + rows.shape[0], field] = rows

    second_sweep(rates, interior, ghosts, columns, inv_y, emit)


def last_kernel(tile_rows, tile0, rates, marks, blocks, interior, ends, inv_y, planes):
    found = ghost_rows([marks[at] for at in range(marks.shape[0])], blocks, tile_rows)
    ghosts = [packed_ghosts(found, field) for field in range(2)]

    def whole(field):
        return interior[:, field].reshape(-1, interior.shape[-1]).astype(F32)

    def emit(field, start, chunk, values):
        count = planes.shape[0]
        for row in range(0, chunk, tile_rows):
            place = ((start + row) // tile_rows + count - tile0) % count
            planes[place, field] = values[row:row + tile_rows]

    second_sweep(rates, whole, ghosts, ends, inv_y, emit)


def cost(flops, nbytes):
    return pl.CostEstimate(flops=flops, bytes_accessed=nbytes, transcendentals=0)


def local(state, inverse_x, inverse_y, rates, partner, face_side, orient, offset):
    magnet = state[0]
    inv_x = inverse_x[0]
    inv_y = inverse_y[0]
    fields, depth, tile_rows, cells = magnet.shape
    lines = inv_y.shape[-1]
    count = lax.axis_size("blk")
    width = lax.axis_size("pen")
    tile0 = (width * 21) // 32
    origin = (count * 9) // 16
    across = turned_group(count, origin)
    within = turned_group(width, tile0)
    numbers = (rates, partner, face_side, orient, offset)
    slots = jax.ShapeDtypeStruct((count, SLOT_ROWS, lines), BF16)
    packed = jax.ShapeDtypeStruct((fields, 16, lines), BF16)
    sweep_flops = 2 * fields * lines * cells * cells
    array_bytes = 2 * fields * lines * cells

    staged, probe = pl.pallas_call(
        stage_kernel,
        out_shape=(
            jax.ShapeDtypeStruct((depth, fields, tile_rows, cells), BF16),
            packed,
        ),
        in_specs=[HBM] * 2,
        out_specs=(VMEM,) * 2,
        scratch_shapes=[
            pltpu.VMEM((fields, 2, 16, cells), BF16),
            pltpu.SemaphoreType.DMA((6,)),
        ],
        compiler_params=pltpu.CompilerParams(vmem_limit_bytes=52 * 1024 * 1024),
        name="stage",
    )(magnet, inv_x)
    moved = lax.all_to_all(staged, "pen", split_axis=0, concat_axis=0, tiled=True, axis_index_groups=within)
    sent, corners = pl.pallas_call(
        functools.partial(layers_kernel, tile0),
        out_shape=(slots, jax.ShapeDtypeStruct((fields, 8, lines), F32)),
        in_specs=[VMEM, VMEM],
        out_specs=(VMEM, VMEM),
        compiler_params=params(),
        cost_estimate=cost(sweep_flops // 16, array_bytes),
        name="layers",
    )(moved, probe)
    blocks = lax.all_to_all(sent, "blk", split_axis=0, concat_axis=0, tiled=True, axis_index_groups=across)
    sent, ghosts = pl.pallas_call(
        functools.partial(next_layers_kernel, tile_rows, origin),
        out_shape=(slots, packed),
        in_specs=[VMEM] * 9,
        out_specs=(VMEM, VMEM),
        compiler_params=params(),
        cost_estimate=cost(sweep_flops // 16, array_bytes),
        name="next_layers",
    )(*numbers, blocks, corners, probe, inv_y)
    blocks = lax.all_to_all(sent, "blk", split_axis=0, concat_axis=0, tiled=True, axis_index_groups=across)
    marks = 3 + (lines // tile_rows).bit_length() - 1
    interior, ends, marks = pl.pallas_call(
        functools.partial(middle_kernel, tile_rows, tile0, origin, count),
        out_shape=(
            jax.ShapeDtypeStruct(moved.shape, BF16),
            packed,
            jax.ShapeDtypeStruct((marks, 8, 128), jnp.int32),
        ),
        input_output_aliases={5: 0},
        in_specs=[VMEM] * 9,
        out_specs=(VMEM, VMEM, VMEM),
        compiler_params=params(),
        cost_estimate=cost(3 * sweep_flops, 4 * array_bytes),
        name="middle",
    )(*numbers, moved, ghosts, inv_y, inv_x)
    planes = pl.pallas_call(
        functools.partial(last_kernel, tile_rows, tile0),
        out_shape=jax.ShapeDtypeStruct((lines // tile_rows, fields, tile_rows, cells), BF16),
        in_specs=[VMEM] * 6,
        out_specs=VMEM,
        compiler_params=params(),
        cost_estimate=cost(sweep_flops, 4 * array_bytes),
        name="last",
    )(rates, marks, blocks, interior, ends, inv_y)
    back = lax.all_to_all(planes, "pen", split_axis=0, concat_axis=0, tiled=True, axis_index_groups=within)
    return from_planes(back)[None]


def solution(mesh):
    return jax.shard_map(
        local,
        mesh=mesh,
        in_specs=(
            P("blk", None, None, "pen", None),
            P("blk", None, None, None),
            P("blk", None, None, None),
            P("blk", None),
            P("blk", None),
            P("blk", None),
            P("blk", None),
            P("blk", None),
        ),
        out_specs=P("blk", None, None, "pen", None),
        check_vma=False,
    )
```
